32 devices in a mesh: grp: 2 (over x), row: 16 (over z, y, core).
Axes of the slice: x: 2, y: 2, z: 4, core: 2. Of those that a mesh axis runs over, the one named last changes fastest.
Arguments:
- excitations: bfloat16 [32, 8192, 128], P('grp', 'row'), parts along dimension 0, may hold values from -0.005859375 to 0.005859375
- valence_orb: bfloat16 [2048, 128], P(('grp', 'row')), parts along dimension 0, may hold values from -6 to 6
- conduction_orb: bfloat16 [2048, 8192], P(('grp', 'row')), parts along dimension 0, may hold values from -6 to 6
- screened: bfloat16 [2048, 1024], P(('grp', 'row')), parts along dimension 0, may hold values from -0.005859375 to 0.005859375
Outputs:
- action: bfloat16 [32, 8192, 128], P('grp', 'row'), parts along dimension 0
The draws below stay inside these ranges and needn't reach their ends.
There are 2 independent parts, one for each index of `grp`. The reference program is written for one: setup_inputs(seed, part) draws one part's arguments, and reference() takes and returns one part's arrays. A program takes and returns all parts, laid end to end along the dimension named above; each array names one. Nothing has to cross between parts.
All inputs are finite; a program needn't handle non-finite values.
Results may differ from the reference program's by a relative error of at most 0.0064.
Values may be sent and summed in bfloat16 or wider, within the bound.
A program may use at most 64 MiB of HBM per device.

```python
import math
import jax
import jax.numpy as jnp
from jax import lax

B = 16
V = 128
C = 8192
P_SIZE = 1024


def shard_levels(own_key, shape, cuts, smallest, high):
    factor_of, own = 1.0, jax.random.fold_in(own_key, 6)
    for axis_at, blocks in cuts:
        heights = jnp.exp(jax.random.uniform(jax.random.fold_in(own, axis_at), (blocks,), jnp.float32, smallest / len(cuts), high / len(cuts)))
        factor_of = factor_of * jnp.repeat(heights, shape[axis_at] // blocks).reshape([-1 if axis == axis_at else 1 for axis in range(len(shape))])
    return factor_of


def gaussian(stream_key, extent, width, bound, pieces=(), held_as=jnp.bfloat16):
    factor_of = shard_levels(stream_key, extent, pieces, -0.22, 0.18) if pieces else 1.0
    drawn = jax.random.normal(stream_key, extent, jnp.float32) * width * factor_of
    return jnp.minimum(jnp.maximum(drawn, -bound), bound).astype(held_as)


def setup_inputs(seed: int = 0, part: int = 0) -> dict:
    arg_keys = jax.random.split(jax.random.key(seed), 5)
    part_keys = jax.random.split(jax.random.fold_in(arg_keys[4], part), 5)
    excitations = gaussian(part_keys[0], (B, C, V), (V * C) ** -0.5, 0.005859375, ((1, 16),))
    valence_orb = gaussian(part_keys[1], (P_SIZE, V), 1.0, 6.0, ((0, 16),))
    conduction_orb = gaussian(part_keys[2], (P_SIZE, C), 1.0, 6.0, ((0, 16),))
    screened = gaussian(part_keys[3], (P_SIZE, P_SIZE), (P_SIZE * P_SIZE) ** -0.5, 0.005859375, ((0, 16),))
    return {"excitations": excitations, "valence_orb": valence_orb, "conduction_orb": conduction_orb, "screened": screened}


def reference(excitations, valence_orb, conduction_orb, screened):
    span_size = math.gcd(P_SIZE, 512)
    block_count = P_SIZE // span_size
    exc = excitations.astype(jnp.float32)
    val_blocks = valence_orb.reshape(block_count, span_size, V)
    cond_blocks = conduction_orb.reshape(block_count, span_size, C)

    def density_block(blocks):
        val_block, cond_block = blocks
        mixed = jnp.einsum("bcv,mv->bmc", exc, val_block.astype(jnp.float32))
        return jnp.sum(mixed * cond_block.astype(jnp.float32)[None], axis=2)

    density = lax.map(density_block, (val_blocks, cond_blocks))
    density = density.transpose(1, 0, 2).reshape(B, P_SIZE).astype(jnp.bfloat16)
    field = jnp.dot(density, screened.T, preferred_element_type=jnp.float32).astype(jnp.bfloat16)
    field_blocks = field.reshape(B, block_count, span_size).transpose(1, 0, 2)

    def project(total, blocks):
        val_block, cond_block, field_block = blocks
        pair = (cond_block.astype(jnp.float32)[None] * field_block.astype(jnp.float32)[:, :, None]).astype(jnp.bfloat16)
        pair = lax.optimization_barrier(pair).astype(jnp.float32)
        total = total + jnp.einsum("bmc,mv->bcv", pair, val_block.astype(jnp.float32))
        return total, None

    initial = jnp.zeros((B, C, V), jnp.float32)
    total, unused = lax.scan(project, initial, (val_blocks, cond_blocks, field_blocks))
    return total.astype(jnp.bfloat16)
```

```python
import functools
import math

import jax
import jax.numpy as jnp
from jax import lax
from jax.experimental import pallas as pl
from jax.experimental.pallas import tpu as pltpu
from jax.sharding import PartitionSpec as P

MESH = pl.DeviceIdType.MESH
NT = (((1,), (1,)), ((), ()))


def flip(index, other, bits):
    total = 0
    for bit in range(bits):
        a = (index // (1 << bit)) % 2
        b = (other // (1 << bit)) % 2
        total = total + (a + b - 2 * a * b) * (1 << bit)
    return total


def send_order(q):
    order = []
    for j in range(q):
        order += [("outer", j), ("near", j)] + ([("plane", j)] if j else [])
    return order + [("centre", j) for j in range(q)]


def gather_kernel(
    n, first_late,
    exc_hbm, val_ref, cond_hbm, scr_ref,
    condt_hbm, valt_hbm, field_hbm,
    condt_ref, valt_ref, field_ref, exc, exct, cond_all, val_all, scr_pair, scr_mixed,
    part, red, early, early_all, late, fld, fld_all,
    exc_sem, own_sem, out_sem, field_sem,
    cond_send, cond_recv, scr_send, scr_recv, va_send, va_recv, vo_send, vo_recv, vb_send, vb_recv,
    part_send, red_recv, early_send, early_recv, late_send, late_recv, fld_send, fld_recv,
):
    rows, cl = val_ref.shape[0], exc.shape[1]
    batch = exc.shape[0]
    q = n // 4
    qbits, bits = q.bit_length() - 1, n.bit_length() - 1
    blocks, bbits = 2 * q, q.bit_length()
    me = lax.axis_index("row")
    my_z, my_q = me // q, me % q
    half = my_z // 2
    outer = (my_z + 1 + half) % 2
    is_outer, is_centre = outer == 1, outer == 0
    mine = half * q + my_q

    exc_copy = pltpu.make_async_copy(exc_hbm, exc, exc_sem)
    exc_copy.start()
    own_val = pltpu.make_async_copy(val_ref, val_all.at[my_q, my_z], own_sem.at[0])
    own_val.start()
    own_scr = pltpu.make_async_copy(scr_ref, scr_pair.at[my_z % 2], own_sem.at[1])
    own_scr.start()
    pltpu.make_async_copy(
        cond_hbm.at[:, pl.ds(pl.multiple_of(me * cl, cl), cl)], cond_all.at[me], cond_recv.at[me]
    ).start()

    barrier = pltpu.get_barrier_semaphore()
    for k in range(1, n):
        pl.semaphore_signal(barrier, inc=1, device_id={"row": flip(me, k, bits)}, device_id_type=MESH)
    pl.semaphore_wait(barrier, n - 1)

    def remote(src, dst, send, recv, to):
        return pltpu.make_async_remote_copy(
            src_ref=src, dst_ref=dst, send_sem=send, recv_sem=recv,
            device_id={"row": to}, device_id_type=MESH,
        )

    def device(kind, j):
        z = {"outer": 3 * (1 - half), "centre": 2 - half, "near": flip(my_z, 1, 2), "plane": my_z}[kind]
        return z * q + flip(my_q, j, qbits)

    sent = []

    def send(*args):
        copy = remote(*args)
        copy.start()
        sent.append(copy)

    send(val_ref, val_all.at[my_q, my_z], va_send.at[0], va_recv.at[my_z], device("centre", 0))
    send(val_ref, val_all.at[my_q, my_z], va_send.at[1], va_recv.at[my_z], device("near", 0))
    for at, (kind, j) in enumerate(send_order(q)):
        to = device(kind, j)
        send(
            cond_hbm.at[:, pl.ds(pl.multiple_of(to * cl, cl), cl)], cond_all.at[me],
            cond_send.at[at], cond_recv.at[me], to,
        )

    scr_copy = remote(scr_ref, scr_pair.at[my_z % 2], scr_send, scr_recv, device("near", 0))

    @pl.when(is_outer)
    def _():
        scr_copy.start()

    exc_copy.wait()

    def turn(b, carry):
        exct[pl.ds(pl.multiple_of(b * 128, 128), 128), :] = exc[b].T
        return carry

    lax.fori_loop(0, batch, turn, 0)

    own_val.wait()
    near_z = flip(my_z, 1, 2)
    far_z = 2 * (1 - half)
    pltpu.make_async_copy(val_ref, val_all.at[my_q, near_z], va_recv.at[near_z]).wait()
    over = remote(
        val_all.at[my_q, pl.ds(far_z, 2)], val_all.at[my_q, pl.ds(far_z, 2)], vo_send, vo_recv, device("near", 0)
    )

    @pl.when(is_centre)
    def _():
        for i in range(2):
            pltpu.make_async_copy(val_ref, val_all.at[my_q, far_z + i], va_recv.at[far_z + i]).wait()
        over.start()

    @pl.when(is_outer)
    def _():
        over.wait_recv()

    for k in range(1, q):
        send(val_all.at[my_q], val_all.at[my_q], vb_send.at[k], vb_recv.at[my_q], device("plane", k))
    for k in range(1, q):
        other = flip(my_q, k, qbits)
        pltpu.make_async_copy(val_all.at[other], val_all.at[other], vb_recv.at[other]).wait()

    def place(step):
        cross, j = (step // q + outer) % 2, step % q
        hh, qq = (half + cross) % 2, flip(my_q, j, qbits)
        direct = jnp.where((outer == 0) & (cross == 1) & (j >= first_late), 1, 0)
        return hh, qq, j, direct

    def to_reducer(step, block):
        return remote(part.at[step], red.at[me], part_send.at[step], red_recv.at[me], q + block)

    def to_centre(step, j, k):
        return remote(
            part.at[step], late.at[mine, j - first_late], late_send.at[j - first_late, k],
            late_recv.at[mine, j - first_late], q + flip(mine, k, bbits),
        )

    def group(step, carry):
        hh, qq, j, direct = place(step)
        block = hh * q + qq
        lanes = pl.ds(pl.multiple_of(block * 2 * rows, 2 * rows), 2 * rows)
        first = 2 * hh * q + qq
        for i in range(2):
            pltpu.make_async_copy(
                cond_all.at[first + i * q], cond_all.at[first + i * q], cond_recv.at[first + i * q]
            ).wait()
        cond = jnp.concatenate([cond_all[first], cond_all[first + q]], axis=0)
        vals = val_all[qq, pl.ds(2 * hh, 2)].reshape(2 * rows, val_ref.shape[1])
        valt = vals.astype(jnp.float32).T
        valt_ref[:, lanes] = valt.astype(jnp.bfloat16)
        mixed = lax.dot_general(exct[...], cond, NT, preferred_element_type=jnp.float32)
        summed = jnp.sum(mixed.reshape(batch, valt.shape[0], 2 * rows) * valt[None], axis=1)
        part[step] = summed.astype(part.dtype)

        @pl.when((direct == 0) & (q + block != me))
        def _():
            to_reducer(step, block).start()

        @pl.when((direct == 0) & (q + block == me))
        def _():
            red[me] = summed.astype(red.dtype)

        @pl.when(direct == 1)
        def _():
            for k in range(1, blocks):
                to_centre(step, j, k).start()
            late[mine, j - first_late] = summed.astype(late.dtype)

        condt_ref[:, lanes] = cond.T
        pltpu.make_async_copy(condt_ref.at[:, lanes], condt_hbm.at[:, lanes], out_sem.at[step, 0]).start()
        pltpu.make_async_copy(valt_ref.at[:, lanes], valt_hbm.at[:, lanes], out_sem.at[step, 1]).start()
        return carry

    lax.fori_loop(0, q, group, 0)
    own_scr.wait()

    @pl.when(is_centre)
    def _():
        other = 1 - my_z % 2
        pltpu.make_async_copy(scr_pair.at[other], scr_pair.at[other], scr_recv).wait()
        whole = scr_pair[...].reshape(2 * rows, scr_ref.shape[1]).astype(jnp.float32)
        for h in range(2):
            for i in range(q):
                first = 2 * h * q + i
                pieces = [whole[:, d * rows:(d + 1) * rows] for d in (first, first + q)]
                at = (h * q + i) * 2 * rows
                scr_mixed[:, at:at + 2 * rows] = jnp.concatenate(pieces, axis=1).astype(jnp.bfloat16)

    lax.fori_loop(q, 2 * q - 1, group, 0)

    def early_copy(k):
        return remote(
            early, early_all.at[mine], early_send.at[k], early_recv.at[mine], q + flip(mine, k, bbits)
        )

    @pl.when(is_centre)
    def _():
        own_outer, own_centre = 3 * half * q, (1 + half) * q
        far_outer, far_centre = 3 * (1 - half) * q, (2 - half) * q
        total = red[me].astype(jnp.float32)
        others = [(own_outer, j) for j in range(q)] + [(own_centre, j) for j in range(1, q)]
        others += [(far_outer, j) for j in range(q)] + [(far_centre, j) for j in range(first_late)]
        for base, j in others:
            other = base + flip(my_q, j, qbits)
            pltpu.make_async_copy(red.at[other], red.at[other], red_recv.at[other]).wait()
            total = total + red[other].astype(jnp.float32)
        early[...] = total.astype(early.dtype)
        early_all[mine] = total.astype(early.dtype)
        for k in range(1, blocks):
            early_copy(k).start()

    group(2 * q - 1, 0)

    def field_copy_to(k):
        return remote(fld, fld_all.at[mine], fld_send.at[k], fld_recv.at[mine], flip(me, k, bits))

    @pl.when(is_centre)
    def _():
        for k in range(1, blocks):
            other = flip(mine, k, bbits)
            pltpu.make_async_copy(early_all.at[other], early_all.at[other], early_recv.at[other]).wait()
        for i in range(q - first_late):
            for k in range(1, blocks):
                other = flip(mine, k, bbits)
                pltpu.make_async_copy(late.at[other, i], late.at[other, i], late_recv.at[other, i]).wait()
        dens = []
        for block in range(blocks):
            total = early_all[block].astype(jnp.float32)
            for j in range(first_late, q):
                source = (1 - block // q) * q + flip(block % q, j, qbits)
                total = total + late[source, j - first_late].astype(jnp.float32)
            dens.append(total)
        whole = jnp.concatenate(dens, axis=1).astype(jnp.bfloat16)
        got = lax.dot_general(whole, scr_mixed[...], NT, preferred_element_type=jnp.float32).astype(jnp.bfloat16)
        fld[...] = got
        fld_all[mine] = got
        for k in range(n - 1, 0, -1):
            field_copy_to(k).start()

    for k in range(1, blocks):
        other = flip(mine, k, bbits)
        pltpu.make_async_copy(fld_all.at[other], fld_all.at[other], fld_recv.at[other]).wait()

    @pl.when(is_outer)
    def _():
        pltpu.make_async_copy(fld_all.at[mine], fld_all.at[mine], fld_recv.at[mine]).wait()

    for block in range(blocks):
        field_ref[:, block * 2 * rows:(block + 1) * 2 * rows] = fld_all[block].astype(jnp.float32)
    field_copy = pltpu.make_async_copy(field_ref, field_hbm, field_sem)
    field_copy.start()

    def finish(step, carry):
        hh, qq, j, direct = place(step)
        block = hh * q + qq
        lanes = pl.ds(pl.multiple_of(block * 2 * rows, 2 * rows), 2 * rows)
        pltpu.make_async_copy(condt_ref.at[:, lanes], condt_hbm.at[:, lanes], out_sem.at[step, 0]).wait()
        pltpu.make_async_copy(valt_ref.at[:, lanes], valt_hbm.at[:, lanes], out_sem.at[step, 1]).wait()

        @pl.when((direct == 0) & (q + block != me))
        def _():
            to_reducer(step, block).wait_send()

        @pl.when(direct == 1)
        def _():
            for k in range(1, blocks):
                to_centre(step, j, k).wait_send()

        return carry

    lax.fori_loop(0, 2 * q, finish, 0)
    for copy in sent:
        copy.wait_send()

    @pl.when(is_outer)
    def _():
        scr_copy.wait_send()

    @pl.when(is_centre)
    def _():
        over.wait_send()
        for k in range(1, blocks):
            early_copy(k).wait_send()
        for k in range(1, n):
            field_copy_to(k).wait_send()

    field_copy.wait()


def project_kernel(condt_hbm, valt_hbm, field_hbm, out_hbm, condt_ref, valt_ref, field_ref, held, in_sem, out_sem):
    loads = [
        pltpu.make_async_copy(src, dst, in_sem.at[at])
        for at, (src, dst) in enumerate(((valt_hbm, valt_ref), (field_hbm, field_ref), (condt_hbm, condt_ref)))
    ]
    for load in loads:
        load.start()
    loads[0].wait()
    loads[1].wait()
    v = valt_ref.shape[0]
    batch = field_ref.shape[0]
    valt = valt_ref[...]
    copies = []
    for b in range(0, batch, 4):
        weights = jnp.concatenate(
            [valt * field_ref[b + i:b + i + 1, :].astype(jnp.bfloat16) for i in range(4)], axis=0
        )
        if b == 0:
            loads[2].wait()
        summed = lax.dot_general(condt_ref[...], weights, NT, preferred_element_type=jnp.float32)
        for i in range(4):
            held[b + i] = summed[:, i * v:(i + 1) * v].astype(jnp.bfloat16)
        copy = pltpu.make_async_copy(held.at[pl.ds(b, 4)], out_hbm.at[pl.ds(b, 4)], out_sem.at[b // 4])
        copy.start()
        copies.append(copy)
    for copy in copies:
        copy.wait()


def fast_body(n, excitations, valence_orb, conduction_orb, screened):
    batch, cl, v = excitations.shape
    rows, points = screened.shape
    q, first_late = n // 4, 1
    blocks, lates = 2 * q, q - first_late
    bf, f32, sent_as = jnp.bfloat16, jnp.float32, jnp.float32
    hbm = pl.BlockSpec(memory_space=pltpu.HBM)
    dma = pltpu.SemaphoreType.DMA
    condt, valt, field = pl.pallas_call(
        functools.partial(gather_kernel, n, first_late),
        out_shape=(
            jax.ShapeDtypeStruct((cl, points), bf),
            jax.ShapeDtypeStruct((v, points), bf),
            jax.ShapeDtypeStruct((batch, points), f32),
        ),
        in_specs=[hbm, hbm, hbm, hbm],
        out_specs=(hbm, hbm, hbm),
        scratch_shapes=[
            pltpu.VMEM((cl, points), bf),
            pltpu.VMEM((v, points), bf),
            pltpu.VMEM((batch, points), f32),
            pltpu.VMEM((batch, cl, v), bf),
            pltpu.VMEM((batch * v, cl), bf),
            pltpu.VMEM((n, rows, cl), bf),
            pltpu.VMEM((q, 4, rows, v), bf),
            pltpu.VMEM((2, rows, points), bf),
            pltpu.VMEM((2 * rows, points), bf),
            pltpu.VMEM((blocks, batch, 2 * rows), sent_as),
            pltpu.VMEM((n, batch, 2 * rows), sent_as),
            pltpu.VMEM((batch, 2 * rows), sent_as),
            pltpu.VMEM((blocks, batch, 2 * rows), sent_as),
            pltpu.VMEM((blocks, lates, batch, 2 * rows), sent_as),
            pltpu.VMEM((batch, 2 * rows), bf),
            pltpu.VMEM((blocks, batch, 2 * rows), bf),
            dma, dma((2,)), dma((blocks, 2)), dma,
            dma((n,)), dma((n,)), dma, dma, dma((2,)), dma((4,)), dma, dma, dma((q,)), dma((q,)),
            dma((blocks,)), dma((n,)), dma((blocks,)), dma((blocks,)),
            dma((lates, blocks)), dma((blocks, lates)), dma((n,)), dma((blocks,)),
        ],
        compiler_params=pltpu.CompilerParams(
            collective_id=0, has_side_effects=True, vmem_limit_bytes=63 * 1024 * 1024
        ),
        name="gather_field",
    )(excitations, valence_orb, conduction_orb, screened)
    return pl.pallas_call(
        project_kernel,
        out_shape=jax.ShapeDtypeStruct((batch, cl, v), bf),
        in_specs=[hbm, hbm, hbm],
        out_specs=hbm,
        scratch_shapes=[
            pltpu.VMEM((cl, points), bf), pltpu.VMEM((v, points), bf), pltpu.VMEM((batch, points), f32),
            pltpu.VMEM((batch, cl, v), bf), dma((3,)), dma((batch // 2,))],
        compiler_params=pltpu.CompilerParams(vmem_limit_bytes=63 * 1024 * 1024),
        name="project",
    )(condt, valt, field)


def over_blocks(total_rows, step_fn, initial):
    span_size = math.gcd(total_rows, 2048)
    block_count = total_rows // span_size
    if block_count == 1:
        return step_fn(initial, 0, span_size)
    return lax.fori_loop(
        0, block_count, lambda index, carry: step_fn(carry, index * span_size, span_size), initial
    )


def density_rows(flat_exc, batch, valence_rows, cond_rows):
    total_rows = valence_rows.shape[0]
    cond_local = cond_rows.shape[1]
    initial = jnp.zeros((batch, total_rows), jnp.float32)

    def step_fn(carry, offset, span_size):
        val_block = lax.dynamic_slice_in_dim(valence_rows, offset, span_size, 0)
        cond_block = lax.dynamic_slice_in_dim(cond_rows, offset, span_size, 0)
        mixed = lax.dot_general(
            flat_exc, val_block, (((1,), (1,)), ((), ())), preferred_element_type=jnp.float32
        )
        mixed = mixed.reshape(batch, cond_local, span_size)
        summed = jnp.sum(mixed * cond_block.T.astype(jnp.float32)[None], axis=1)
        return lax.dynamic_update_slice_in_dim(carry, summed, offset, 1)

    return over_blocks(total_rows, step_fn, initial)


def projection(carry, valence_rows, cond_rows, field_cols):
    total_rows = valence_rows.shape[0]
    batch = field_cols.shape[0]
    cond_local = cond_rows.shape[1]

    def step_fn(inner, offset, span_size):
        val_block = lax.dynamic_slice_in_dim(valence_rows, offset, span_size, 0)
        cond_block = lax.dynamic_slice_in_dim(cond_rows, offset, span_size, 0)
        field_block = lax.dynamic_slice_in_dim(field_cols, offset, span_size, 1)
        pair = (
            cond_block.T.astype(jnp.float32)[None] * field_block.astype(jnp.float32)[:, None, :]
        ).astype(jnp.bfloat16)
        pair = pair.reshape(batch * cond_local, span_size)
        return inner + jnp.dot(pair, val_block, preferred_element_type=jnp.float32)

    return over_blocks(total_rows, step_fn, carry)


def general_body(excitations, valence_orb, conduction_orb, screened):
    batch, cond_local, valence = excitations.shape
    flat_exc = excitations.reshape(batch * cond_local, valence)
    valence_whole = lax.all_gather(valence_orb, "row", axis=0, tiled=True)
    cond_rows = lax.all_to_all(conduction_orb, "row", split_axis=1, concat_axis=0, tiled=True)
    partial_density = density_rows(flat_exc, batch, valence_whole, cond_rows)
    density_whole = lax.psum(partial_density, "row").astype(jnp.bfloat16)
    field_mine = lax.dot_general(
        density_whole, screened, (((1,), (1,)), ((), ())), preferred_element_type=jnp.float32
    ).astype(jnp.bfloat16)
    initial = jnp.zeros((batch * cond_local, valence), jnp.float32)
    summed = projection(
        initial, valence_whole, cond_rows, lax.all_gather(field_mine, "row", axis=1, tiled=True)
    )
    return summed.reshape(batch, cond_local, valence).astype(jnp.bfloat16)


def body(n, excitations, valence_orb, conduction_orb, screened):
    batch, cl, v = excitations.shape
    rows = valence_orb.shape[0]
    fits = n == 16 and cl % 128 == 0 and v == 128 and rows == 64 and batch == 16
    if fits:
        return fast_body(n, excitations, valence_orb, conduction_orb, screened)
    return general_body(excitations, valence_orb, conduction_orb, screened)


def solution(mesh):
    in_specs = (
        P("grp", "row", None),
        P(("grp", "row"), None),
        P(("grp", "row"), None),
        P(("grp", "row"), None),
    )
    out_specs = P("grp", "row", None)
    return jax.shard_map(
        functools.partial(body, mesh.shape["row"]),
        mesh=mesh, in_specs=in_specs, out_specs=out_specs, check_vma=False,
    )
```

```python
import functools
import math

import jax
import jax.numpy as jnp
from jax import lax
from jax.experimental import pallas as pl
from jax.experimental.pallas import tpu as pltpu
from jax.sharding import PartitionSpec as P

MESH = pl.DeviceIdType.MESH
NT = (((1,), (1,)), ((), ()))


def flip(index, other, bits):
    total = 0
    for bit in range(bits):
        a = (index // (1 << bit)) % 2
        b = (other // (1 << bit)) % 2
        total = total + (a + b - 2 * a * b) * (1 << bit)
    return total


def send_order(q):
    order = []
    for j in range(q):
        order += [("outer", j), ("near", j)] + ([("plane", j)] if j else [])
    return order + [("centre", j) for j in range(q)]


def gather_kernel(
    n, first_late,
    exc_hbm, val_ref, cond_hbm, scr_ref,
    condt_hbm, valt_hbm, field_hbm,
    condt_ref, valt_ref, field_ref, exc, exct, cond_all, val_all, scr_pair, scr_mixed,
    part, red, early, early_all, late, fld, fld_all,
    exc_sem, own_sem, out_sem, field_sem,
    cond_send, cond_recv, scr_send, scr_recv, va_send, va_recv, vb_send, vb_recv,
    part_send, red_recv, early_send, early_recv, late_send, late_recv, fld_send, fld_recv,
):
    rows, cl = val_ref.shape[0], exc.shape[1]
    batch = exc.shape[0]
    q = n // 4
    qbits, bits = q.bit_length() - 1, n.bit_length() - 1
    blocks, bbits = 2 * q, q.bit_length()
    me = lax.axis_index("row")
    my_z, my_q = me // q, me % q
    half = my_z // 2
    outer = (my_z + 1 + half) % 2
    is_outer, is_centre = outer == 1, outer == 0
    mine = half * q + my_q

    exc_copy = pltpu.make_async_copy(exc_hbm, exc, exc_sem)
    exc_copy.start()
    own_val = pltpu.make_async_copy(val_ref, val_all.at[my_q, my_z], own_sem.at[0])
    own_val.start()
    own_scr = pltpu.make_async_copy(scr_ref, scr_pair.at[my_z % 2], own_sem.at[1])
    own_scr.start()
    pltpu.make_async_copy(
        cond_hbm.at[:, pl.ds(pl.multiple_of(me * cl, cl), cl)], cond_all.at[me], cond_recv.at[me]
    ).start()

    barrier = pltpu.get_barrier_semaphore()
    for k in range(1, n):
        pl.semaphore_signal(barrier, inc=1, device_id={"row": flip(me, k, bits)}, device_id_type=MESH)
    pl.semaphore_wait(barrier, n - 1)

    def remote(src, dst, send, recv, to):
        return pltpu.make_async_remote_copy(
            src_ref=src, dst_ref=dst, send_sem=send, recv_sem=recv,
            device_id={"row": to}, device_id_type=MESH,
        )

    def device(kind, j):
        z = {"outer": 3 * (1 - half), "centre": 2 - half, "near": flip(my_z, 1, 2), "plane": my_z}[kind]
        return z * q + flip(my_q, j, qbits)

    sent = []

    def send(*args):
        copy = remote(*args)
        copy.start()
        sent.append(copy)

    for at, kind in enumerate(("outer", "centre", "near")):
        send(val_ref, val_all.at[my_q, my_z], va_send.at[at], va_recv.at[my_z], device(kind, 0))
    for at, (kind, j) in enumerate(send_order(q)):
        to = device(kind, j)
        send(
            cond_hbm.at[:, pl.ds(pl.multiple_of(to * cl, cl), cl)], cond_all.at[me],
            cond_send.at[at], cond_recv.at[me], to,
        )

    scr_copy = remote(scr_ref, scr_pair.at[my_z % 2], scr_send, scr_recv, device("near", 0))

    @pl.when(is_outer)
    def _():
        scr_copy.start()

    exc_copy.wait()

    def turn(b, carry):
        exct[pl.ds(pl.multiple_of(b * 128, 128), 128), :] = exc[b].T
        return carry

    lax.fori_loop(0, batch, turn, 0)

    own_val.wait()
    for k in range(1, 4):
        z = flip(my_z, k, 2)
        pltpu.make_async_copy(val_ref, val_all.at[my_q, z], va_recv.at[z]).wait()
    for k in range(1, q):
        send(val_all.at[my_q], val_all.at[my_q], vb_send.at[k], vb_recv.at[my_q], device("plane", k))
    for k in range(1, q):
        other = flip(my_q, k, qbits)
        pltpu.make_async_copy(val_all.at[other], val_all.at[other], vb_recv.at[other]).wait()

    def place(step):
        cross, j = (step // q + outer) % 2, step % q
        hh, qq = (half + cross) % 2, flip(my_q, j, qbits)
        direct = jnp.where((outer == 0) & (cross == 1) & (j >= first_late), 1, 0)
        return hh, qq, j, direct

    def to_reducer(step, block):
        return remote(part.at[step], red.at[me], part_send.at[step], red_recv.at[me], q + block)

    def to_centre(step, j, k):
        return remote(
            part.at[step], late.at[mine, j - first_late], late_send.at[j - first_late, k],
            late_recv.at[mine, j - first_late], q + flip(mine, k, bbits),
        )

    def group(step, carry):
        hh, qq, j, direct = place(step)
        block = hh * q + qq
        lanes = pl.ds(pl.multiple_of(block * 2 * rows, 2 * rows), 2 * rows)
        first = 2 * hh * q + qq
        for i in range(2):
            pltpu.make_async_copy(
                cond_all.at[first + i * q], cond_all.at[first + i * q], cond_recv.at[first + i * q]
            ).wait()
        cond = jnp.concatenate([cond_all[first], cond_all[first + q]], axis=0)
        vals = val_all[qq, pl.ds(2 * hh, 2)].reshape(2 * rows, val_ref.shape[1])
        valt = vals.astype(jnp.float32).T
        valt_ref[:, lanes] = valt.astype(jnp.bfloat16)
        mixed = lax.dot_general(exct[...], cond, NT, preferred_element_type=jnp.float32)
        summed = jnp.sum(mixed.reshape(batch, valt.shape[0], 2 * rows) * valt[None], axis=1)
        part[step] = summed.astype(part.dtype)

        @pl.when((direct == 0) & (q + block != me))
        def _():
            to_reducer(step, block).start()

        @pl.when((direct == 0) & (q + block == me))
        def _():
            red[me] = summed.astype(red.dtype)

        @pl.when(direct == 1)
        def _():
            for k in range(1, blocks):
                to_centre(step, j, k).start()
            late[mine, j - first_late] = summed.astype(late.dtype)

        condt_ref[:, lanes] = cond.T
        pltpu.make_async_copy(condt_ref.at[:, lanes], condt_hbm.at[:, lanes], out_sem.at[step, 0]).start()
        pltpu.make_async_copy(valt_ref.at[:, lanes], valt_hbm.at[:, lanes], out_sem.at[step, 1]).start()
        return carry

    lax.fori_loop(0, q, group, 0)
    own_scr.wait()

    @pl.when(is_centre)
    def _():
        other = 1 - my_z % 2
        pltpu.make_async_copy(scr_pair.at[other], scr_pair.at[other], scr_recv).wait()
        whole = scr_pair[...].reshape(2 * rows, scr_ref.shape[1]).astype(jnp.float32)
        for h in range(2):
            for i in range(q):
                first = 2 * h * q + i
                pieces = [whole[:, d * rows:(d + 1) * rows] for d in (first, first + q)]
                at = (h * q + i) * 2 * rows
                scr_mixed[:, at:at + 2 * rows] = jnp.concatenate(pieces, axis=1).astype(jnp.bfloat16)

    lax.fori_loop(q, 2 * q - 1, group, 0)

    def early_copy(k):
        return remote(
            early, early_all.at[mine], early_send.at[k], early_recv.at[mine], q + flip(mine, k, bbits)
        )

    @pl.when(is_centre)
    def _():
        own_outer, own_centre = 3 * half * q, (1 + half) * q
        far_outer, far_centre = 3 * (1 - half) * q, (2 - half) * q
        total = red[me].astype(jnp.float32)
        others = [(own_outer, j) for j in range(q)] + [(own_centre, j) for j in range(1, q)]
        others += [(far_outer, j) for j in range(q)] + [(far_centre, j) for j in range(first_late)]
        for base, j in others:
            other = base + flip(my_q, j, qbits)
            pltpu.make_async_copy(red.at[other], red.at[other], red_recv.at[other]).wait()
            total = total + red[other].astype(jnp.float32)
        early[...] = total.astype(early.dtype)
        early_all[mine] = total.astype(early.dtype)
        for k in range(1, blocks):
            early_copy(k).start()

    group(2 * q - 1, 0)

    def field_copy_to(k):
        return remote(fld, fld_all.at[mine], fld_send.at[k], fld_recv.at[mine], flip(me, k, bits))

    @pl.when(is_centre)
    def _():
        for k in range(1, blocks):
            other = flip(mine, k, bbits)
            pltpu.make_async_copy(early_all.at[other], early_all.at[other], early_recv.at[other]).wait()
        for i in range(q - first_late):
            for k in range(1, blocks):
                other = flip(mine, k, bbits)
                pltpu.make_async_copy(late.at[other, i], late.at[other, i], late_recv.at[other, i]).wait()
        dens = []
        for block in range(blocks):
            total = early_all[block].astype(jnp.float32)
            for j in range(first_late, q):
                source = (1 - block // q) * q + flip(block % q, j, qbits)
                total = total + late[source, j - first_late].astype(jnp.float32)
            dens.append(total)
        whole = jnp.concatenate(dens, axis=1).astype(jnp.bfloat16)
        got = lax.dot_general(whole, scr_mixed[...], NT, preferred_element_type=jnp.float32).astype(jnp.bfloat16)
        fld[...] = got
        fld_all[mine] = got
        for k in range(n - 1, 0, -1):
            field_copy_to(k).start()

    for k in range(1, blocks):
        other = flip(mine, k, bbits)
        pltpu.make_async_copy(fld_all.at[other], fld_all.at[other], fld_recv.at[other]).wait()

    @pl.when(is_outer)
    def _():
        pltpu.make_async_copy(fld_all.at[mine], fld_all.at[mine], fld_recv.at[mine]).wait()

    for block in range(blocks):
        field_ref[:, block * 2 * rows:(block + 1) * 2 * rows] = fld_all[block].astype(jnp.float32)
    field_copy = pltpu.make_async_copy(field_ref, field_hbm, field_sem)
    field_copy.start()

    def finish(step, carry):
        hh, qq, j, direct = place(step)
        block = hh * q + qq
        lanes = pl.ds(pl.multiple_of(block * 2 * rows, 2 * rows), 2 * rows)
        pltpu.make_async_copy(condt_ref.at[:, lanes], condt_hbm.at[:, lanes], out_sem.at[step, 0]).wait()
        pltpu.make_async_copy(valt_ref.at[:, lanes], valt_hbm.at[:, lanes], out_sem.at[step, 1]).wait()

        @pl.when((direct == 0) & (q + block != me))
        def _():
            to_reducer(step, block).wait_send()

        @pl.when(direct == 1)
        def _():
            for k in range(1, blocks):
                to_centre(step, j, k).wait_send()

        return carry

    lax.fori_loop(0, 2 * q, finish, 0)
    for copy in sent:
        copy.wait_send()

    @pl.when(is_outer)
    def _():
        scr_copy.wait_send()

    @pl.when(is_centre)
    def _():
        for k in range(1, blocks):
            early_copy(k).wait_send()
        for k in range(1, n):
            field_copy_to(k).wait_send()

    field_copy.wait()


def project_kernel(condt_hbm, valt_hbm, field_hbm, out_hbm, condt_ref, valt_ref, field_ref, held, in_sem, out_sem):
    loads = [
        pltpu.make_async_copy(src, dst, in_sem.at[at])
        for at, (src, dst) in enumerate(((valt_hbm, valt_ref), (field_hbm, field_ref), (condt_hbm, condt_ref)))
    ]
    for load in loads:
        load.start()
    loads[0].wait()
    loads[1].wait()
    v = valt_ref.shape[0]
    batch = field_ref.shape[0]
    valt = valt_ref[...]
    copies = []
    for b in range(0, batch, 4):
        weights = jnp.concatenate(
            [valt * field_ref[b + i:b + i + 1, :].astype(jnp.bfloat16) for i in range(4)], axis=0
        )
        if b == 0:
            loads[2].wait()
        summed = lax.dot_general(condt_ref[...], weights, NT, preferred_element_type=jnp.float32)
        for i in range(4):
            held[b + i] = summed[:, i * v:(i + 1) * v].astype(jnp.bfloat16)
        copy = pltpu.make_async_copy(held.at[pl.ds(b, 4)], out_hbm.at[pl.ds(b, 4)], out_sem.at[b // 4])
        copy.start()
        copies.append(copy)
    for copy in copies:
        copy.wait()


def fast_body(n, excitations, valence_orb, conduction_orb, screened):
    batch, cl, v = excitations.shape
    rows, points = screened.shape
    q, first_late = n // 4, 1
    blocks, lates = 2 * q, q - first_late
    bf, f32, sent_as = jnp.bfloat16, jnp.float32, jnp.float32
    hbm = pl.BlockSpec(memory_space=pltpu.HBM)
    dma = pltpu.SemaphoreType.DMA
    condt, valt, field = pl.pallas_call(
        functools.partial(gather_kernel, n, first_late),
        out_shape=(
            jax.ShapeDtypeStruct((cl, points), bf),
            jax.ShapeDtypeStruct((v, points), bf),
            jax.ShapeDtypeStruct((batch, points), f32),
        ),
        in_specs=[hbm, hbm, hbm, hbm],
        out_specs=(hbm, hbm, hbm),
        scratch_shapes=[
            pltpu.VMEM((cl, points), bf),
            pltpu.VMEM((v, points), bf),
            pltpu.VMEM((batch, points), f32),
            pltpu.VMEM((batch, cl, v), bf),
            pltpu.VMEM((batch * v, cl), bf),
            pltpu.VMEM((n, rows, cl), bf),
            pltpu.VMEM((q, 4, rows, v), bf),
            pltpu.VMEM((2, rows, points), bf),
            pltpu.VMEM((2 * rows, points), bf),
            pltpu.VMEM((blocks, batch, 2 * rows), sent_as),
            pltpu.VMEM((n, batch, 2 * rows), sent_as),
            pltpu.VMEM((batch, 2 * rows), sent_as),
            pltpu.VMEM((blocks, batch, 2 * rows), sent_as),
            pltpu.VMEM((blocks, lates, batch, 2 * rows), sent_as),
            pltpu.VMEM((batch, 2 * rows), bf),
            pltpu.VMEM((blocks, batch, 2 * rows), bf),
            dma, dma((2,)), dma((blocks, 2)), dma,
            dma((n,)), dma((n,)), dma, dma, dma((3,)), dma((4,)), dma((q,)), dma((q,)),
            dma((blocks,)), dma((n,)), dma((blocks,)), dma((blocks,)),
            dma((lates, blocks)), dma((blocks, lates)), dma((n,)), dma((blocks,)),
        ],
        compiler_params=pltpu.CompilerParams(
            collective_id=0, has_side_effects=True, vmem_limit_bytes=63 * 1024 * 1024
        ),
        name="gather_field",
    )(excitations, valence_orb, conduction_orb, screened)
    return pl.pallas_call(
        project_kernel,
        out_shape=jax.ShapeDtypeStruct((batch, cl, v), bf),
        in_specs=[hbm, hbm, hbm],
        out_specs=hbm,
        scratch_shapes=[
            pltpu.VMEM((cl, points), bf), pltpu.VMEM((v, points), bf), pltpu.VMEM((batch, points), f32),
            pltpu.VMEM((batch, cl, v), bf), dma((3,)), dma((batch // 2,))],
        compiler_params=pltpu.CompilerParams(vmem_limit_bytes=63 * 1024 * 1024),
        name="project",
    )(condt, valt, field)


def over_blocks(total_rows, step_fn, initial):
    span_size = math.gcd(total_rows, 2048)
    block_count = total_rows // span_size
    if block_count == 1:
        return step_fn(initial, 0, span_size)
    return lax.fori_loop(
        0, block_count, lambda index, carry: step_fn(carry, index * span_size, span_size), initial
    )


def density_rows(flat_exc, batch, valence_rows, cond_rows):
    total_rows = valence_rows.shape[0]
    cond_local = cond_rows.shape[1]
    initial = jnp.zeros((batch, total_rows), jnp.float32)

    def step_fn(carry, offset, span_size):
        val_block = lax.dynamic_slice_in_dim(valence_rows, offset, span_size, 0)
        cond_block = lax.dynamic_slice_in_dim(cond_rows, offset, span_size, 0)
        mixed = lax.dot_general(
            flat_exc, val_block, (((1,), (1,)), ((), ())), preferred_element_type=jnp.float32
        )
        mixed = mixed.reshape(batch, cond_local, span_size)
        summed = jnp.sum(mixed * cond_block.T.astype(jnp.float32)[None], axis=1)
        return lax.dynamic_update_slice_in_dim(carry, summed, offset, 1)

    return over_blocks(total_rows, step_fn, initial)


def projection(carry, valence_rows, cond_rows, field_cols):
    total_rows = valence_rows.shape[0]
    batch = field_cols.shape[0]
    cond_local = cond_rows.shape[1]

    def step_fn(inner, offset, span_size):
        val_block = lax.dynamic_slice_in_dim(valence_rows, offset, span_size, 0)
        cond_block = lax.dynamic_slice_in_dim(cond_rows, offset, span_size, 0)
        field_block = lax.dynamic_slice_in_dim(field_cols, offset, span_size, 1)
        pair = (
            cond_block.T.astype(jnp.float32)[None] * field_block.astype(jnp.float32)[:, None, :]
        ).astype(jnp.bfloat16)
        pair = pair.reshape(batch * cond_local, span_size)
        return inner + jnp.dot(pair, val_block, preferred_element_type=jnp.float32)

    return over_blocks(total_rows, step_fn, carry)


def general_body(excitations, valence_orb, conduction_orb, screened):
    batch, cond_local, valence = excitations.shape
    flat_exc = excitations.reshape(batch * cond_local, valence)
    valence_whole = lax.all_gather(valence_orb, "row", axis=0, tiled=True)
    cond_rows = lax.all_to_all(conduction_orb, "row", split_axis=1, concat_axis=0, tiled=True)
    partial_density = density_rows(flat_exc, batch, valence_whole, cond_rows)
    density_whole = lax.psum(partial_density, "row").astype(jnp.bfloat16)
    field_mine = lax.dot_general(
        density_whole, screened, (((1,), (1,)), ((), ())), preferred_element_type=jnp.float32
    ).astype(jnp.bfloat16)
    initial = jnp.zeros((batch * cond_local, valence), jnp.float32)
    summed = projection(
        initial, valence_whole, cond_rows, lax.all_gather(field_mine, "row", axis=1, tiled=True)
    )
    return summed.reshape(batch, cond_local, valence).astype(jnp.bfloat16)


def body(n, excitations, valence_orb, conduction_orb, screened):
    batch, cl, v = excitations.shape
    rows = valence_orb.shape[0]
    fits = n == 16 and cl % 128 == 0 and v == 128 and rows == 64 and batch == 16
    if fits:
        return fast_body(n, excitations, valence_orb, conduction_orb, screened)
    return general_body(excitations, valence_orb, conduction_orb, screened)


def solution(mesh):
    in_specs = (
        P("grp", "row", None),
        P(("grp", "row"), None),
        P(("grp", "row"), None),
        P(("grp", "row"), None),
    )
    out_specs = P("grp", "row", None)
    return jax.shard_map(
        functools.partial(body, mesh.shape["row"]),
        mesh=mesh, in_specs=in_specs, out_specs=out_specs, check_vma=False,
    )
```

```python
import functools
import math

import jax
import jax.numpy as jnp
from jax import lax
from jax.experimental import pallas as pl
from jax.experimental.pallas import tpu as pltpu
from jax.sharding import PartitionSpec as P

MESH = pl.DeviceIdType.MESH
NT = (((1,), (1,)), ((), ()))


def flip(index, other, bits):
    total = 0
    for bit in range(bits):
        a = (index // (1 << bit)) % 2
        b = (other // (1 << bit)) % 2
        total = total + (a + b - 2 * a * b) * (1 << bit)
    return total


def send_order(q):
    order = []
    for j in range(q):
        order += [("outer", j), ("near", j)] + ([("plane", j)] if j else [])
    return order + [("centre", j) for j in range(q)]


def gather_kernel(
    n, first_late,
    exc_hbm, val_ref, cond_hbm, scr_ref,
    condt_ref, valt_ref, field_ref, exc, exct, cond_all, val_all, scr_pair, scr_mixed,
    part, red, early, early_all, late, fld, fld_all,
    exc_sem, own_sem,
    cond_send, cond_recv, scr_send, scr_recv, va_send, va_recv, vb_send, vb_recv,
    part_send, red_recv, early_send, early_recv, late_send, late_recv, fld_send, fld_recv,
):
    rows, cl = val_ref.shape[0], exc.shape[1]
    batch = exc.shape[0]
    q = n // 4
    qbits, bits = q.bit_length() - 1, n.bit_length() - 1
    blocks, bbits = 2 * q, q.bit_length()
    me = lax.axis_index("row")
    my_z, my_q = me // q, me % q
    half = my_z // 2
    outer = (my_z + 1 + half) % 2
    is_outer, is_centre = outer == 1, outer == 0
    mine = half * q + my_q

    exc_copy = pltpu.make_async_copy(exc_hbm, exc, exc_sem)
    exc_copy.start()
    own_val = pltpu.make_async_copy(val_ref, val_all.at[my_q, my_z], own_sem.at[0])
    own_val.start()
    own_scr = pltpu.make_async_copy(scr_ref, scr_pair.at[my_z % 2], own_sem.at[1])
    own_scr.start()
    pltpu.make_async_copy(
        cond_hbm.at[:, pl.ds(pl.multiple_of(me * cl, cl), cl)], cond_all.at[me], cond_recv.at[me]
    ).start()

    barrier = pltpu.get_barrier_semaphore()
    for k in range(1, n):
        pl.semaphore_signal(barrier, inc=1, device_id={"row": flip(me, k, bits)}, device_id_type=MESH)
    pl.semaphore_wait(barrier, n - 1)

    def remote(src, dst, send, recv, to):
        return pltpu.make_async_remote_copy(
            src_ref=src, dst_ref=dst, send_sem=send, recv_sem=recv,
            device_id={"row": to}, device_id_type=MESH,
        )

    def device(kind, j):
        z = {"outer": 3 * (1 - half), "centre": 2 - half, "near": flip(my_z, 1, 2), "plane": my_z}[kind]
        return z * q + flip(my_q, j, qbits)

    sent = []

    def send(*args):
        copy = remote(*args)
        copy.start()
        sent.append(copy)

    for at, kind in enumerate(("outer", "centre", "near")):
        send(val_ref, val_all.at[my_q, my_z], va_send.at[at], va_recv.at[my_z], device(kind, 0))
    for at, (kind, j) in enumerate(send_order(q)):
        to = device(kind, j)
        send(
            cond_hbm.at[:, pl.ds(pl.multiple_of(to * cl, cl), cl)], cond_all.at[me],
            cond_send.at[at], cond_recv.at[me], to,
        )

    scr_copy = remote(scr_ref, scr_pair.at[my_z % 2], scr_send, scr_recv, device("near", 0))

    @pl.when(is_outer)
    def _():
        scr_copy.start()

    exc_copy.wait()

    def turn(b, carry):
        exct[pl.ds(pl.multiple_of(b * 128, 128), 128), :] = exc[b].T
        return carry

    lax.fori_loop(0, batch, turn, 0)

    own_val.wait()
    for k in range(1, 4):
        z = flip(my_z, k, 2)
        pltpu.make_async_copy(val_ref, val_all.at[my_q, z], va_recv.at[z]).wait()
    for k in range(1, q):
        send(val_all.at[my_q], val_all.at[my_q], vb_send.at[k], vb_recv.at[my_q], device("plane", k))
    for k in range(1, q):
        other = flip(my_q, k, qbits)
        pltpu.make_async_copy(val_all.at[other], val_all.at[other], vb_recv.at[other]).wait()

    def place(step):
        cross, j = (step // q + outer) % 2, step % q
        hh, qq = (half + cross) % 2, flip(my_q, j, qbits)
        direct = jnp.where((outer == 0) & (cross == 1) & (j >= first_late), 1, 0)
        return hh, qq, j, direct

    def to_reducer(step, block):
        return remote(part.at[step], red.at[me], part_send.at[step], red_recv.at[me], q + block)

    def to_centre(step, j, k):
        return remote(
            part.at[step], late.at[mine, j - first_late], late_send.at[j - first_late, k],
            late_recv.at[mine, j - first_late], q + flip(mine, k, bbits),
        )

    def group(step, carry):
        hh, qq, j, direct = place(step)
        block = hh * q + qq
        lanes = pl.ds(pl.multiple_of(block * 2 * rows, 2 * rows), 2 * rows)
        first = 2 * hh * q + qq
        for i in range(2):
            pltpu.make_async_copy(
                cond_all.at[first + i * q], cond_all.at[first + i * q], cond_recv.at[first + i * q]
            ).wait()
        cond = jnp.concatenate([cond_all[first], cond_all[first + q]], axis=0)
        vals = val_all[qq, pl.ds(2 * hh, 2)].reshape(2 * rows, val_ref.shape[1])
        valt = vals.astype(jnp.float32).T
        valt_ref[:, lanes] = valt.astype(jnp.bfloat16)
        mixed = lax.dot_general(exct[...], cond, NT, preferred_element_type=jnp.float32)
        summed = jnp.sum(mixed.reshape(batch, valt.shape[0], 2 * rows) * valt[None], axis=1)
        part[step] = summed.astype(part.dtype)

        @pl.when((direct == 0) & (q + block != me))
        def _():
            to_reducer(step, block).start()

        @pl.when((direct == 0) & (q + block == me))
        def _():
            red[me] = summed.astype(red.dtype)

        @pl.when(direct == 1)
        def _():
            for k in range(1, blocks):
                to_centre(step, j, k).start()
            late[mine, j - first_late] = summed.astype(late.dtype)

        condt_ref[:, lanes] = cond.T
        return carry

    lax.fori_loop(0, q, group, 0)
    own_scr.wait()

    @pl.when(is_centre)
    def _():
        other = 1 - my_z % 2
        pltpu.make_async_copy(scr_pair.at[other], scr_pair.at[other], scr_recv).wait()
        whole = scr_pair[...].reshape(2 * rows, scr_ref.shape[1]).astype(jnp.float32)
        for h in range(2):
            for i in range(q):
                first = 2 * h * q + i
                pieces = [whole[:, d * rows:(d + 1) * rows] for d in (first, first + q)]
                at = (h * q + i) * 2 * rows
                scr_mixed[:, at:at + 2 * rows] = jnp.concatenate(pieces, axis=1).astype(jnp.bfloat16)

    lax.fori_loop(q, 2 * q - 1, group, 0)

    def early_copy(k):
        return remote(
            early, early_all.at[mine], early_send.at[k], early_recv.at[mine], q + flip(mine, k, bbits)
        )

    @pl.when(is_centre)
    def _():
        own_outer, own_centre = 3 * half * q, (1 + half) * q
        far_outer, far_centre = 3 * (1 - half) * q, (2 - half) * q
        total = red[me].astype(jnp.float32)
        others = [(own_outer, j) for j in range(q)] + [(own_centre, j) for j in range(1, q)]
        others += [(far_outer, j) for j in range(q)] + [(far_centre, j) for j in range(first_late)]
        for base, j in others:
            other = base + flip(my_q, j, qbits)
            pltpu.make_async_copy(red.at[other], red.at[other], red_recv.at[other]).wait()
            total = total + red[other].astype(jnp.float32)
        early[...] = total.astype(early.dtype)
        early_all[mine] = total.astype(early.dtype)
        for k in range(1, blocks):
            early_copy(k).start()

    group(2 * q - 1, 0)

    def field_copy_to(k):
        return remote(fld, fld_all.at[mine], fld_send.at[k], fld_recv.at[mine], flip(me, k, bits))

    @pl.when(is_centre)
    def _():
        for k in range(1, blocks):
            other = flip(mine, k, bbits)
            pltpu.make_async_copy(early_all.at[other], early_all.at[other], early_recv.at[other]).wait()
        for i in range(q - first_late):
            for k in range(1, blocks):
                other = flip(mine, k, bbits)
                pltpu.make_async_copy(late.at[other, i], late.at[other, i], late_recv.at[other, i]).wait()
        dens = []
        for block in range(blocks):
            total = early_all[block].astype(jnp.float32)
            for j in range(first_late, q):
                source = (1 - block // q) * q + flip(block % q, j, qbits)
                total = total + late[source, j - first_late].astype(jnp.float32)
            dens.append(total)
        whole = jnp.concatenate(dens, axis=1).astype(jnp.bfloat16)
        got = lax.dot_general(whole, scr_mixed[...], NT, preferred_element_type=jnp.float32).astype(jnp.bfloat16)
        fld[...] = got
        fld_all[mine] = got
        for k in range(n - 1, 0, -1):
            field_copy_to(k).start()

    for k in range(1, blocks):
        other = flip(mine, k, bbits)
        pltpu.make_async_copy(fld_all.at[other], fld_all.at[other], fld_recv.at[other]).wait()

    @pl.when(is_outer)
    def _():
        pltpu.make_async_copy(fld_all.at[mine], fld_all.at[mine], fld_recv.at[mine]).wait()

    for block in range(blocks):
        field_ref[:, block * 2 * rows:(block + 1) * 2 * rows] = fld_all[block].astype(jnp.float32)

    def finish(step, carry):
        hh, qq, j, direct = place(step)
        block = hh * q + qq

        @pl.when((direct == 0) & (q + block != me))
        def _():
            to_reducer(step, block).wait_send()

        @pl.when(direct == 1)
        def _():
            for k in range(1, blocks):
                to_centre(step, j, k).wait_send()

        return carry

    lax.fori_loop(0, 2 * q, finish, 0)
    for copy in sent:
        copy.wait_send()

    @pl.when(is_outer)
    def _():
        scr_copy.wait_send()

    @pl.when(is_centre)
    def _():
        for k in range(1, blocks):
            early_copy(k).wait_send()
        for k in range(1, n):
            field_copy_to(k).wait_send()


def project_kernel(condt_ref, valt_ref, field_ref, out_hbm, held, out_sem):
    v = valt_ref.shape[0]
    batch = field_ref.shape[0]
    valt = valt_ref[...]
    copies = []
    for b in range(0, batch, 4):
        weights = jnp.concatenate(
            [valt * field_ref[b + i:b + i + 1, :].astype(jnp.bfloat16) for i in range(4)], axis=0
        )
        summed = lax.dot_general(condt_ref[...], weights, NT, preferred_element_type=jnp.float32)
        for i in range(4):
            held[b + i] = summed[:, i * v:(i + 1) * v].astype(jnp.bfloat16)
        copy = pltpu.make_async_copy(held.at[pl.ds(b, 4)], out_hbm.at[pl.ds(b, 4)], out_sem.at[b // 4])
        copy.start()
        copies.append(copy)
    for copy in copies:
        copy.wait()


def fast_body(n, excitations, valence_orb, conduction_orb, screened):
    batch, cl, v = excitations.shape
    rows, points = screened.shape
    q, first_late = n // 4, 2
    blocks, lates = 2 * q, q - first_late
    bf, f32, sent_as = jnp.bfloat16, jnp.float32, jnp.float32
    hbm = pl.BlockSpec(memory_space=pltpu.HBM)
    vmem = pl.BlockSpec(memory_space=pltpu.VMEM)
    dma = pltpu.SemaphoreType.DMA
    condt, valt, field = pl.pallas_call(
        functools.partial(gather_kernel, n, first_late),
        out_shape=(
            jax.ShapeDtypeStruct((cl, points), bf),
            jax.ShapeDtypeStruct((v, points), bf),
            jax.ShapeDtypeStruct((batch, points), f32),
        ),
        in_specs=[hbm, hbm, hbm, hbm],
        out_specs=(vmem, vmem, vmem),
        scratch_shapes=[
            pltpu.VMEM((batch, cl, v), bf),
            pltpu.VMEM((batch * v, cl), bf),
            pltpu.VMEM((n, rows, cl), bf),
            pltpu.VMEM((q, 4, rows, v), bf),
            pltpu.VMEM((2, rows, points), bf),
            pltpu.VMEM((2 * rows, points), bf),
            pltpu.VMEM((blocks, batch, 2 * rows), sent_as),
            pltpu.VMEM((n, batch, 2 * rows), sent_as),
            pltpu.VMEM((batch, 2 * rows), sent_as),
            pltpu.VMEM((blocks, batch, 2 * rows), sent_as),
            pltpu.VMEM((blocks, lates, batch, 2 * rows), sent_as),
            pltpu.VMEM((batch, 2 * rows), bf),
            pltpu.VMEM((blocks, batch, 2 * rows), bf),
            dma, dma((2,)),
            dma((n,)), dma((n,)), dma, dma, dma((3,)), dma((4,)), dma((q,)), dma((q,)),
            dma((blocks,)), dma((n,)), dma((blocks,)), dma((blocks,)),
            dma((lates, blocks)), dma((blocks, lates)), dma((n,)), dma((blocks,)),
        ],
        compiler_params=pltpu.CompilerParams(
            collective_id=0, has_side_effects=True, vmem_limit_bytes=24 * 1024 * 1024
        ),
        name="gather_field",
    )(*[pltpu.with_memory_space_constraint(x, pltpu.HBM) for x in (excitations, valence_orb, conduction_orb, screened)])
    return pl.pallas_call(
        project_kernel,
        out_shape=jax.ShapeDtypeStruct((batch, cl, v), bf),
        in_specs=[vmem, vmem, vmem],
        out_specs=hbm,
        scratch_shapes=[pltpu.VMEM((batch, cl, v), bf), dma((batch // 4,))],
        compiler_params=pltpu.CompilerParams(vmem_limit_bytes=24 * 1024 * 1024),
        name="project",
    )(condt, valt, field)


def over_blocks(total_rows, step_fn, initial):
    span_size = math.gcd(total_rows, 2048)
    block_count = total_rows // span_size
    if block_count == 1:
        return step_fn(initial, 0, span_size)
    return lax.fori_loop(
        0, block_count, lambda index, carry: step_fn(carry, index * span_size, span_size), initial
    )


def density_rows(flat_exc, batch, valence_rows, cond_rows):
    total_rows = valence_rows.shape[0]
    cond_local = cond_rows.shape[1]
    initial = jnp.zeros((batch, total_rows), jnp.float32)

    def step_fn(carry, offset, span_size):
        val_block = lax.dynamic_slice_in_dim(valence_rows, offset, span_size, 0)
        cond_block = lax.dynamic_slice_in_dim(cond_rows, offset, span_size, 0)
        mixed = lax.dot_general(
            flat_exc, val_block, (((1,), (1,)), ((), ())), preferred_element_type=jnp.float32
        )
        mixed = mixed.reshape(batch, cond_local, span_size)
        summed = jnp.sum(mixed * cond_block.T.astype(jnp.float32)[None], axis=1)
        return lax.dynamic_update_slice_in_dim(carry, summed, offset, 1)

    return over_blocks(total_rows, step_fn, initial)


def projection(carry, valence_rows, cond_rows, field_cols):
    total_rows = valence_rows.shape[0]
    batch = field_cols.shape[0]
    cond_local = cond_rows.shape[1]

    def step_fn(inner, offset, span_size):
        val_block = lax.dynamic_slice_in_dim(valence_rows, offset, span_size, 0)
        cond_block = lax.dynamic_slice_in_dim(cond_rows, offset, span_size, 0)
        field_block = lax.dynamic_slice_in_dim(field_cols, offset, span_size, 1)
        pair = (
            cond_block.T.astype(jnp.float32)[None] * field_block.astype(jnp.float32)[:, None, :]
        ).astype(jnp.bfloat16)
        pair = pair.reshape(batch * cond_local, span_size)
        return inner + jnp.dot(pair, val_block, preferred_element_type=jnp.float32)

    return over_blocks(total_rows, step_fn, carry)


def general_body(excitations, valence_orb, conduction_orb, screened):
    batch, cond_local, valence = excitations.shape
    flat_exc = excitations.reshape(batch * cond_local, valence)
    valence_whole = lax.all_gather(valence_orb, "row", axis=0, tiled=True)
    cond_rows = lax.all_to_all(conduction_orb, "row", split_axis=1, concat_axis=0, tiled=True)
    partial_density = density_rows(flat_exc, batch, valence_whole, cond_rows)
    density_whole = lax.psum(partial_density, "row").astype(jnp.bfloat16)
    field_mine = lax.dot_general(
        density_whole, screened, (((1,), (1,)), ((), ())), preferred_element_type=jnp.float32
    ).astype(jnp.bfloat16)
    initial = jnp.zeros((batch * cond_local, valence), jnp.float32)
    summed = projection(
        initial, valence_whole, cond_rows, lax.all_gather(field_mine, "row", axis=1, tiled=True)
    )
    return summed.reshape(batch, cond_local, valence).astype(jnp.bfloat16)


def body(n, excitations, valence_orb, conduction_orb, screened):
    batch, cl, v = excitations.shape
    rows = valence_orb.shape[0]
    fits = n == 16 and cl % 128 == 0 and v == 128 and rows == 64 and batch == 16
    if fits:
        return fast_body(n, excitations, valence_orb, conduction_orb, screened)
    return general_body(excitations, valence_orb, conduction_orb, screened)


def solution(mesh):
    in_specs = (
        P("grp", "row", None),
        P(("grp", "row"), None),
        P(("grp", "row"), None),
        P(("grp", "row"), None),
    )
    out_specs = P("grp", "row", None)
    return jax.shard_map(
        functools.partial(body, mesh.shape["row"]),
        mesh=mesh, in_specs=in_specs, out_specs=out_specs, check_vma=False,
    )
```

```python
import functools
import math

import jax
import jax.numpy as jnp
from jax import lax
from jax.experimental import pallas as pl
from jax.experimental.pallas import tpu as pltpu
from jax.sharding import PartitionSpec as P

MESH = pl.DeviceIdType.MESH
NT = (((1,), (1,)), ((), ()))


def flip(index, other, bits):
    total = 0
    for bit in range(bits):
        a = (index // (1 << bit)) % 2
        b = (other // (1 << bit)) % 2
        total = total + (a + b - 2 * a * b) * (1 << bit)
    return total


KINDS = ("outer", "centre", "near", "plane")


def gather_kernel(
    n, first_late,
    exc_hbm, val_ref, cond_hbm, scr_ref,
    condt_ref, valt_ref, field_ref, exc, exct, cond_all, val_all, scr_pair, scr_mixed,
    part, red, early, early_all, late, fld, fld_all,
    exc_sem, own_sem,
    cond_send, cond_recv, scr_send, scr_recv, va_send, va_recv, vb_send, vb_recv,
    part_send, red_recv, early_send, early_recv, late_send, late_recv, fld_send, fld_recv,
):
    rows, cl = val_ref.shape[0], exc.shape[1]
    batch = exc.shape[0]
    q = n // 4
    qbits, bits = q.bit_length() - 1, n.bit_length() - 1
    blocks, bbits = 2 * q, q.bit_length()
    me = lax.axis_index("row")
    my_z, my_q = me // q, me % q
    half = my_z // 2
    outer = (my_z + 1 + half) % 2
    is_outer, is_centre = outer == 1, outer == 0
    mine = half * q + my_q

    barrier = pltpu.get_barrier_semaphore()
    for k in range(n - 1, 0, -1):
        to = flip(me, k, bits)

        pl.semaphore_signal(barrier, inc=1, device_id={"row": to}, device_id_type=MESH)

    exc_copy = pltpu.make_async_copy(exc_hbm, exc, exc_sem)
    exc_copy.start()
    own_val = pltpu.make_async_copy(val_ref, val_all.at[my_q, my_z], own_sem.at[0])
    own_val.start()
    own_scr = pltpu.make_async_copy(scr_ref, scr_pair.at[my_z % 2], own_sem.at[1])
    own_scr.start()
    pltpu.make_async_copy(
        cond_hbm.at[:, pl.ds(pl.multiple_of(me * cl, cl), cl)], cond_all.at[me], cond_recv.at[me]
    ).start()
    pl.semaphore_wait(barrier, n - 1)

    def remote(src, dst, send, recv, to):
        return pltpu.make_async_remote_copy(
            src_ref=src, dst_ref=dst, send_sem=send, recv_sem=recv,
            device_id={"row": to}, device_id_type=MESH,
        )

    def device(kind, j):
        z = {"outer": 3 * (1 - half), "centre": 2 - half, "near": flip(my_z, 1, 2), "plane": my_z}[kind]
        return z * q + flip(my_q, j, qbits)

    def block_to(kind, j):
        to = device(kind, j)
        return remote(
            cond_hbm.at[:, pl.ds(pl.multiple_of(to * cl, cl), cl)], cond_all.at[me],
            cond_send.at[KINDS.index(kind) * q + j], cond_recv.at[me], to,
        )

    def val_to(at, kind):
        return remote(val_ref, val_all.at[my_q, my_z], va_send.at[at], va_recv.at[my_z], device(kind, 0))

    scr_copy = remote(scr_ref, scr_pair.at[my_z % 2], scr_send, scr_recv, device("near", 0))

    val_to(0, "outer").start()
    val_to(1, "centre").start()
    val_to(2, "near").start()
    for j in range(q):
        block_to("outer", j).start()


    exc_copy.wait()

    def turn(b, carry):
        exct[pl.ds(pl.multiple_of(b * 128, 128), 128), :] = exc[b].T
        return carry

    lax.fori_loop(0, batch, turn, 0)

    own_val.wait()
    def val_wait(z):
        pltpu.make_async_copy(val_ref, val_all.at[my_q, z], va_recv.at[z]).wait()

    def share(k):
        return remote(val_all.at[my_q], val_all.at[my_q], vb_send.at[k], vb_recv.at[my_q], device("plane", k))

    for k in range(1, 4):
        val_wait(flip(my_z, k, 2))
    for k in range(1, q):
        share(k).start()
    for j in range(1, q):
        block_to("plane", j).start()
    for j in range(q):
        block_to("near", j).start()

    @pl.when(is_centre)
    def _():
        for j in range(q):
            block_to("centre", j).start()

    @pl.when(is_outer)
    def _():
        scr_copy.start()

    for k in range(1, q):
        other = flip(my_q, k, qbits)
        pltpu.make_async_copy(val_all.at[other], val_all.at[other], vb_recv.at[other]).wait()

    def place(step):
        cross, j = (step // q + outer) % 2, step % q
        hh, qq = (half + cross) % 2, flip(my_q, j, qbits)
        direct = jnp.where((outer == 0) & (cross == 1) & (j >= first_late), 1, 0)
        return hh, qq, j, direct

    def to_reducer(step, block):
        return remote(part.at[step], red.at[me], part_send.at[step], red_recv.at[me], q + block)

    def to_centre(step, j, k):
        return remote(
            part.at[step], late.at[mine, j - first_late], late_send.at[j - first_late, k],
            late_recv.at[mine, j - first_late], q + flip(mine, k, bbits),
        )

    def group(step, carry):
        hh, qq, j, direct = place(step)
        block = hh * q + qq
        lanes = pl.ds(pl.multiple_of(block * 2 * rows, 2 * rows), 2 * rows)
        first = 2 * hh * q + qq
        for i in range(2):
            pltpu.make_async_copy(
                cond_all.at[first + i * q], cond_all.at[first + i * q], cond_recv.at[first + i * q]
            ).wait()
        cond = jnp.concatenate([cond_all[first], cond_all[first + q]], axis=0)
        vals = val_all[qq, pl.ds(2 * hh, 2)].reshape(2 * rows, val_ref.shape[1])
        valt = vals.astype(jnp.float32).T
        valt_ref[:, lanes] = valt.astype(jnp.bfloat16)
        mixed = lax.dot_general(exct[...], cond, NT, preferred_element_type=jnp.float32)
        summed = jnp.sum(mixed.reshape(batch, valt.shape[0], 2 * rows) * valt[None], axis=1)
        part[step] = summed.astype(part.dtype)

        @pl.when((direct == 0) & (q + block != me))
        def _():
            to_reducer(step, block).start()

        @pl.when((direct == 0) & (q + block == me))
        def _():
            red[me] = summed.astype(red.dtype)

        @pl.when(direct == 1)
        def _():
            for k in range(1, blocks):
                to_centre(step, j, k).start()
            late[mine, j - first_late] = summed.astype(late.dtype)

        condt_ref[:, lanes] = cond.T
        return carry

    lax.fori_loop(0, q, group, 0)
    @pl.when(is_outer)
    def _():
        for j in range(q):
            block_to("centre", j).start()

    own_scr.wait()

    @pl.when(is_centre)
    def _():
        other = 1 - my_z % 2
        pltpu.make_async_copy(scr_pair.at[other], scr_pair.at[other], scr_recv).wait()
        whole = scr_pair[...].reshape(2 * rows, scr_ref.shape[1]).astype(jnp.float32)
        for h in range(2):
            for i in range(q):
                first = 2 * h * q + i
                pieces = [whole[:, d * rows:(d + 1) * rows] for d in (first, first + q)]
                at = (h * q + i) * 2 * rows
                scr_mixed[at:at + 2 * rows, :] = jnp.concatenate(pieces, axis=1).T.astype(jnp.bfloat16)

    lax.fori_loop(q, 2 * q - 1, group, 0)

    def early_copy(k):
        return remote(
            early, early_all.at[mine], early_send.at[k], early_recv.at[mine], q + flip(mine, k, bbits)
        )

    @pl.when(is_centre)
    def _():
        own_outer, own_centre = 3 * half * q, (1 + half) * q
        far_outer, far_centre = 3 * (1 - half) * q, (2 - half) * q
        total = red[me].astype(jnp.float32)
        others = [(own_outer, j) for j in range(q)] + [(own_centre, j) for j in range(1, q)]
        others += [(far_outer, j) for j in range(q)] + [(far_centre, j) for j in range(first_late)]
        for base, j in others:
            other = base + flip(my_q, j, qbits)
            pltpu.make_async_copy(red.at[other], red.at[other], red_recv.at[other]).wait()
            total = total + red[other].astype(jnp.float32)
        early[...] = total.astype(early.dtype)
        early_all[mine] = total.astype(early.dtype)
        for k in range(1, blocks):
            early_copy(k).start()

    group(2 * q - 1, 0)

    def field_copy_to(k):
        return remote(fld, fld_all.at[mine], fld_send.at[k], fld_recv.at[mine], flip(me, k, bits))

    @pl.when(is_centre)
    def _():
        for k in range(1, blocks):
            other = flip(mine, k, bbits)
            pltpu.make_async_copy(early_all.at[other], early_all.at[other], early_recv.at[other]).wait()
        for i in range(q - first_late):
            for k in range(1, blocks):
                other = flip(mine, k, bbits)
                pltpu.make_async_copy(late.at[other, i], late.at[other, i], late_recv.at[other, i]).wait()
        dens = []
        for block in range(blocks):
            total = early_all[block].astype(jnp.float32)
            for j in range(first_late, q):
                source = (1 - block // q) * q + flip(block % q, j, qbits)
                total = total + late[source, j - first_late].astype(jnp.float32)
            dens.append(total)
        whole = jnp.concatenate(dens, axis=1).astype(jnp.bfloat16)
        got = jnp.dot(whole, scr_mixed[...], preferred_element_type=jnp.float32).astype(jnp.bfloat16)
        fld[...] = got
        fld_all[mine] = got
        for k in range(n - 1, 0, -1):
            field_copy_to(k).start()

    for k in range(1, blocks):
        other = flip(mine, k, bbits)
        pltpu.make_async_copy(fld_all.at[other], fld_all.at[other], fld_recv.at[other]).wait()

    @pl.when(is_outer)
    def _():
        pltpu.make_async_copy(fld_all.at[mine], fld_all.at[mine], fld_recv.at[mine]).wait()

    for block in range(blocks):
        field_ref[:, block * 2 * rows:(block + 1) * 2 * rows] = fld_all[block].astype(jnp.float32)

    def finish(step, carry):
        hh, qq, j, direct = place(step)
        block = hh * q + qq

        @pl.when((direct == 0) & (q + block != me))
        def _():
            to_reducer(step, block).wait_send()

        @pl.when(direct == 1)
        def _():
            for k in range(1, blocks):
                to_centre(step, j, k).wait_send()

        return carry

    lax.fori_loop(0, 2 * q, finish, 0)
    for kind in KINDS:
        for j in range(1 if kind == "plane" else 0, q):
            block_to(kind, j).wait_send()
    for at, kind in enumerate(("outer", "centre", "near")):
        val_to(at, kind).wait_send()
    for k in range(1, q):
        share(k).wait_send()

    @pl.when(is_outer)
    def _():
        scr_copy.wait_send()

    @pl.when(is_centre)
    def _():
        for k in range(1, blocks):
            early_copy(k).wait_send()
        for k in range(1, n):
            field_copy_to(k).wait_send()


def project_kernel(condt_ref, valt_ref, field_ref, out_hbm, held, out_sem):
    v = valt_ref.shape[0]
    batch = field_ref.shape[0]
    valt = valt_ref[...]
    copies = []
    for b in range(0, batch, 4):
        weights = jnp.concatenate(
            [valt * field_ref[b + i:b + i + 1, :].astype(jnp.bfloat16) for i in range(4)], axis=0
        )
        summed = lax.dot_general(condt_ref[...], weights, NT, preferred_element_type=jnp.float32)
        for i in range(4):
            held[b + i] = summed[:, i * v:(i + 1) * v].astype(jnp.bfloat16)
        copy = pltpu.make_async_copy(held.at[pl.ds(b, 4)], out_hbm.at[pl.ds(b, 4)], out_sem.at[b // 4])
        copy.start()
        copies.append(copy)
    for copy in copies:
        copy.wait()


def fast_body(n, excitations, valence_orb, conduction_orb, screened):
    batch, cl, v = excitations.shape
    rows, points = screened.shape
    q, first_late = n // 4, 2
    blocks, lates = 2 * q, q - first_late
    bf, f32, sent_as = jnp.bfloat16, jnp.float32, jnp.bfloat16
    hbm = pl.BlockSpec(memory_space=pltpu.HBM)
    vmem = pl.BlockSpec(memory_space=pltpu.VMEM)
    dma = pltpu.SemaphoreType.DMA
    condt, valt, field = pl.pallas_call(
        functools.partial(gather_kernel, n, first_late),
        out_shape=(
            jax.ShapeDtypeStruct((cl, points), bf),
            jax.ShapeDtypeStruct((v, points), bf),
            jax.ShapeDtypeStruct((batch, points), f32),
        ),
        in_specs=[hbm, hbm, hbm, hbm],
        out_specs=(vmem, vmem, vmem),
        scratch_shapes=[
            pltpu.VMEM((batch, cl, v), bf),
            pltpu.VMEM((batch * v, cl), bf),
            pltpu.VMEM((n, rows, cl), bf),
            pltpu.VMEM((q, 4, rows, v), bf),
            pltpu.VMEM((2, rows, points), bf),
            pltpu.VMEM((points, 2 * rows), bf),
            pltpu.VMEM((blocks, batch, 2 * rows), sent_as),
            pltpu.VMEM((n, batch, 2 * rows), sent_as),
            pltpu.VMEM((batch, 2 * rows), f32),
            pltpu.VMEM((blocks, batch, 2 * rows), f32),
            pltpu.VMEM((blocks, lates, batch, 2 * rows), sent_as),
            pltpu.VMEM((batch, 2 * rows), bf),
            pltpu.VMEM((blocks, batch, 2 * rows), bf),
            dma, dma((2,)),
            dma((n,)), dma((n,)), dma, dma, dma((3,)), dma((4,)), dma((q,)), dma((q,)),
            dma((blocks,)), dma((n,)), dma((blocks,)), dma((blocks,)),
            dma((lates, blocks)), dma((blocks, lates)), dma((n,)), dma((blocks,)),
        ],
        compiler_params=pltpu.CompilerParams(
            collective_id=0, has_side_effects=True, vmem_limit_bytes=24 * 1024 * 1024
        ),
        name="gather_field",
    )(*[pltpu.with_memory_space_constraint(x, pltpu.HBM) for x in (excitations, valence_orb, conduction_orb, screened)])
    return pl.pallas_call(
        project_kernel,
        out_shape=jax.ShapeDtypeStruct((batch, cl, v), bf),
        in_specs=[vmem, vmem, vmem],
        out_specs=hbm,
        scratch_shapes=[pltpu.VMEM((batch, cl, v), bf), dma((batch // 4,))],
        compiler_params=pltpu.CompilerParams(vmem_limit_bytes=24 * 1024 * 1024),
        name="project",
    )(condt, valt, field)


def over_blocks(total_rows, step_fn, initial):
    span_size = math.gcd(total_rows, 2048)
    block_count = total_rows // span_size
    if block_count == 1:
        return step_fn(initial, 0, span_size)
    return lax.fori_loop(
        0, block_count, lambda index, carry: step_fn(carry, index * span_size, span_size), initial
    )


def density_rows(flat_exc, batch, valence_rows, cond_rows):
    total_rows = valence_rows.shape[0]
    cond_local = cond_rows.shape[1]
    initial = jnp.zeros((batch, total_rows), jnp.float32)

    def step_fn(carry, offset, span_size):
        val_block = lax.dynamic_slice_in_dim(valence_rows, offset, span_size, 0)
        cond_block = lax.dynamic_slice_in_dim(cond_rows, offset, span_size, 0)
        mixed = lax.dot_general(
            flat_exc, val_block, (((1,), (1,)), ((), ())), preferred_element_type=jnp.float32
        )
        mixed = mixed.reshape(batch, cond_local, span_size)
        summed = jnp.sum(mixed * cond_block.T.astype(jnp.float32)[None], axis=1)
        return lax.dynamic_update_slice_in_dim(carry, summed, offset, 1)

    return over_blocks(total_rows, step_fn, initial)


def projection(carry, valence_rows, cond_rows, field_cols):
    total_rows = valence_rows.shape[0]
    batch = field_cols.shape[0]
    cond_local = cond_rows.shape[1]

    def step_fn(inner, offset, span_size):
        val_block = lax.dynamic_slice_in_dim(valence_rows, offset, span_size, 0)
        cond_block = lax.dynamic_slice_in_dim(cond_rows, offset, span_size, 0)
        field_block = lax.dynamic_slice_in_dim(field_cols, offset, span_size, 1)
        pair = (
            cond_block.T.astype(jnp.float32)[None] * field_block.astype(jnp.float32)[:, None, :]
        ).astype(jnp.bfloat16)
        pair = pair.reshape(batch * cond_local, span_size)
        return inner + jnp.dot(pair, val_block, preferred_element_type=jnp.float32)

    return over_blocks(total_rows, step_fn, carry)


def general_body(excitations, valence_orb, conduction_orb, screened):
    batch, cond_local, valence = excitations.shape
    flat_exc = excitations.reshape(batch * cond_local, valence)
    valence_whole = lax.all_gather(valence_orb, "row", axis=0, tiled=True)
    cond_rows = lax.all_to_all(conduction_orb, "row", split_axis=1, concat_axis=0, tiled=True)
    partial_density = density_rows(flat_exc, batch, valence_whole, cond_rows)
    density_whole = lax.psum(partial_density, "row").astype(jnp.bfloat16)
    field_mine = lax.dot_general(
        density_whole, screened, (((1,), (1,)), ((), ())), preferred_element_type=jnp.float32
    ).astype(jnp.bfloat16)
    initial = jnp.zeros((batch * cond_local, valence), jnp.float32)
    summed = projection(
        initial, valence_whole, cond_rows, lax.all_gather(field_mine, "row", axis=1, tiled=True)
    )
    return summed.reshape(batch, cond_local, valence).astype(jnp.bfloat16)


def body(n, excitations, valence_orb, conduction_orb, screened):
    batch, cl, v = excitations.shape
    rows = valence_orb.shape[0]
    fits = n == 16 and cl % 128 == 0 and v == 128 and rows == 64 and batch == 16
    if fits:
        return fast_body(n, excitations, valence_orb, conduction_orb, screened)
    return general_body(excitations, valence_orb, conduction_orb, screened)


def solution(mesh):
    in_specs = (
        P("grp", "row", None),
        P(("grp", "row"), None),
        P(("grp", "row"), None),
        P(("grp", "row"), None),
    )
    out_specs = P("grp", "row", None)
    return jax.shard_map(
        functools.partial(body, mesh.shape["row"]),
        mesh=mesh, in_specs=in_specs, out_specs=out_specs, check_vma=False,
    )
```

```python
import functools
import math

import jax
import jax.numpy as jnp
from jax import lax
from jax.experimental import pallas as pl
from jax.experimental.pallas import tpu as pltpu
from jax.sharding import PartitionSpec as P

MESH = pl.DeviceIdType.MESH
NT = (((1,), (1,)), ((), ()))


def flip(index, other, bits):
    total = 0
    for bit in range(bits):
        a = (index // (1 << bit)) % 2
        b = (other // (1 << bit)) % 2
        total = total + (a + b - 2 * a * b) * (1 << bit)
    return total


KINDS = ("outer", "centre", "near", "plane")


def gather_kernel(
    n, first_late,
    exc_hbm, val_ref, cond_hbm, scr_ref,
    condt_ref, valt_ref, field_ref, exc, exct, cond_all, val_all, scr_pair, scr_mixed,
    part, red, early, early_all, late, fld, fld_all,
    exc_sem, own_sem,
    cond_send, cond_recv, scr_send, scr_recv, va_send, va_recv, vb_send, vb_recv,
    part_send, red_recv, early_send, early_recv, late_send, late_recv, fld_send, fld_recv,
):
    rows, cl = val_ref.shape[0], exc.shape[1]
    batch = exc.shape[0]
    q = n // 4
    qbits, bits = q.bit_length() - 1, n.bit_length() - 1
    blocks, bbits = 2 * q, q.bit_length()
    me = lax.axis_index("row")
    my_z, my_q = me // q, me % q
    half = my_z // 2
    outer = (my_z + 1 + half) % 2
    is_outer, is_centre = outer == 1, outer == 0
    mine = half * q + my_q

    barrier = pltpu.get_barrier_semaphore()
    for k in range(n - 1, 0, -1):
        to = flip(me, k, bits)

        pl.semaphore_signal(barrier, inc=1, device_id={"row": to}, device_id_type=MESH)

    exc_copy = pltpu.make_async_copy(exc_hbm, exc, exc_sem)
    exc_copy.start()
    own_val = pltpu.make_async_copy(val_ref, val_all.at[my_q, my_z], own_sem.at[0])
    own_val.start()
    own_scr = pltpu.make_async_copy(scr_ref, scr_pair.at[my_z % 2], own_sem.at[1])
    own_scr.start()
    pltpu.make_async_copy(
        cond_hbm.at[:, pl.ds(pl.multiple_of(me * cl, cl), cl)], cond_all.at[me], cond_recv.at[me]
    ).start()
    pl.semaphore_wait(barrier, n - 1)

    def remote(src, dst, send, recv, to):
        return pltpu.make_async_remote_copy(
            src_ref=src, dst_ref=dst, send_sem=send, recv_sem=recv,
            device_id={"row": to}, device_id_type=MESH,
        )

    def device(kind, j):
        z = {"outer": 3 * (1 - half), "centre": 2 - half, "near": flip(my_z, 1, 2), "plane": my_z}[kind]
        return z * q + flip(my_q, j, qbits)

    def block_to(kind, j):
        to = device(kind, j)
        return remote(
            cond_hbm.at[:, pl.ds(pl.multiple_of(to * cl, cl), cl)], cond_all.at[me],
            cond_send.at[KINDS.index(kind) * q + j], cond_recv.at[me], to,
        )

    def val_to(at, kind):
        return remote(val_ref, val_all.at[my_q, my_z], va_send.at[at], va_recv.at[my_z], device(kind, 0))

    scr_copy = remote(scr_ref, scr_pair.at[my_z % 2], scr_send, scr_recv, device("near", 0))

    val_to(0, "outer").start()
    val_to(1, "centre").start()
    val_to(2, "near").start()
    for j in range(q):
        block_to("outer", j).start()


    exc_copy.wait()

    def turn(b, carry):
        exct[pl.ds(pl.multiple_of(b * 128, 128), 128), :] = exc[b].T
        return carry

    lax.fori_loop(0, batch, turn, 0)

    own_val.wait()
    def val_wait(z):
        pltpu.make_async_copy(val_ref, val_all.at[my_q, z], va_recv.at[z]).wait()

    def share(k):
        return remote(val_all.at[my_q], val_all.at[my_q], vb_send.at[k], vb_recv.at[my_q], device("plane", k))

    for k in range(1, 4):
        val_wait(flip(my_z, k, 2))
    for k in range(1, q):
        share(k).start()
    for j in range(1, q):
        block_to("plane", j).start()
    for j in range(q):
        block_to("near", j).start()

    @pl.when(is_centre)
    def _():
        for j in range(q):
            block_to("centre", j).start()

    @pl.when(is_outer)
    def _():
        scr_copy.start()

    for k in range(1, q):
        other = flip(my_q, k, qbits)
        pltpu.make_async_copy(val_all.at[other], val_all.at[other], vb_recv.at[other]).wait()

    def place(step):
        cross, j = (step // q + outer) % 2, step % q
        hh, qq = (half + cross) % 2, flip(my_q, j, qbits)
        direct = jnp.where((outer == 0) & (cross == 1) & (j >= first_late), 1, 0)
        return hh, qq, j, direct

    def to_reducer(step, block):
        return remote(part.at[step], red.at[me], part_send.at[step], red_recv.at[me], q + block)

    def to_centre(step, j, k):
        return remote(
            part.at[step], late.at[mine, j - first_late], late_send.at[j - first_late, k],
            late_recv.at[mine, j - first_late], q + flip(mine, k, bbits),
        )

    def group(step, carry):
        hh, qq, j, direct = place(step)
        block = hh * q + qq
        lanes = pl.ds(pl.multiple_of(block * 2 * rows, 2 * rows), 2 * rows)
        first = 2 * hh * q + qq
        for i in range(2):
            pltpu.make_async_copy(
                cond_all.at[first + i * q], cond_all.at[first + i * q], cond_recv.at[first + i * q]
            ).wait()
        cond = jnp.concatenate([cond_all[first], cond_all[first + q]], axis=0)
        vals = val_all[qq, pl.ds(2 * hh, 2)].reshape(2 * rows, val_ref.shape[1])
        valt = vals.astype(jnp.float32).T
        valt_ref[:, lanes] = valt.astype(jnp.bfloat16)
        mixed = lax.dot_general(exct[...], cond, NT, preferred_element_type=jnp.float32)
        summed = jnp.sum(mixed.reshape(batch, valt.shape[0], 2 * rows) * valt[None], axis=1)
        part[step] = summed.astype(part.dtype)

        @pl.when((direct == 0) & (q + block != me))
        def _():
            to_reducer(step, block).start()

        @pl.when((direct == 0) & (q + block == me))
        def _():
            red[me] = summed.astype(red.dtype)

        @pl.when(direct == 1)
        def _():
            for k in range(blocks - 1, 0, -1):
                to_centre(step, j, k).start()
            late[mine, j - first_late] = summed.astype(late.dtype)

        condt_ref[:, lanes] = cond.T

        @pl.when((outer == 1) & (step < q))
        def _():
            block_to("centre", step).start()

        return carry

    lax.fori_loop(0, q, group, 0)

    own_scr.wait()

    @pl.when(is_centre)
    def _():
        other = 1 - my_z % 2
        pltpu.make_async_copy(scr_pair.at[other], scr_pair.at[other], scr_recv).wait()
        whole = scr_pair[...].reshape(2 * rows, scr_ref.shape[1]).astype(jnp.float32)
        for h in range(2):
            for i in range(q):
                first = 2 * h * q + i
                pieces = [whole[:, d * rows:(d + 1) * rows] for d in (first, first + q)]
                at = (h * q + i) * 2 * rows
                scr_mixed[at:at + 2 * rows, :] = jnp.concatenate(pieces, axis=1).T.astype(jnp.bfloat16)

    lax.fori_loop(q, 2 * q - 1, group, 0)

    def early_copy(k):
        return remote(
            early, early_all.at[mine], early_send.at[k], early_recv.at[mine], q + flip(mine, k, bbits)
        )

    @pl.when(is_centre)
    def _():
        own_outer, own_centre = 3 * half * q, (1 + half) * q
        far_outer, far_centre = 3 * (1 - half) * q, (2 - half) * q
        total = red[me].astype(jnp.float32)
        others = [(own_outer, j) for j in range(q)] + [(own_centre, j) for j in range(1, q)]
        others += [(far_outer, j) for j in range(q)] + [(far_centre, j) for j in range(first_late)]
        for base, j in others:
            other = base + flip(my_q, j, qbits)
            pltpu.make_async_copy(red.at[other], red.at[other], red_recv.at[other]).wait()
            total = total + red[other].astype(jnp.float32)
        early[...] = total.astype(early.dtype)
        early_all[mine] = total.astype(early.dtype)
        for k in range(blocks - 1, 0, -1):
            early_copy(k).start()

    group(2 * q - 1, 0)

    def field_copy_to(k):
        return remote(fld, fld_all.at[mine], fld_send.at[k], fld_recv.at[mine], k)

    @pl.when(is_centre)
    def _():
        for k in range(1, blocks):
            other = flip(mine, k, bbits)
            pltpu.make_async_copy(early_all.at[other], early_all.at[other], early_recv.at[other]).wait()
        dens = [early_all[block].astype(jnp.float32) for block in range(blocks)]
        for j in range(first_late, q):
            at = j - first_late
            for k in range(1, blocks):
                other = flip(mine, k, bbits)
                pltpu.make_async_copy(late.at[other, at], late.at[other, at], late_recv.at[other, at]).wait()
            for block in range(blocks):
                source = (1 - block // q) * q + flip(block % q, j, qbits)
                dens[block] = dens[block] + late[source, at].astype(jnp.float32)
        whole = jnp.concatenate(dens, axis=1).astype(jnp.bfloat16)
        got = jnp.dot(whole, scr_mixed[...], preferred_element_type=jnp.float32).astype(jnp.bfloat16)
        fld[...] = got
        fld_all[mine] = got
        for to in [*range(q), *range(3 * q, n), *range(2 * q, 3 * q), *range(q, 2 * q)]:
            @pl.when(to != me)
            def _():
                field_copy_to(to).start()

    for k in range(1, blocks):
        other = flip(mine, k, bbits)
        pltpu.make_async_copy(fld_all.at[other], fld_all.at[other], fld_recv.at[other]).wait()

    @pl.when(is_outer)
    def _():
        pltpu.make_async_copy(fld_all.at[mine], fld_all.at[mine], fld_recv.at[mine]).wait()

    for block in range(blocks):
        field_ref[:, block * 2 * rows:(block + 1) * 2 * rows] = fld_all[block].astype(jnp.float32)

    def finish(step, carry):
        hh, qq, j, direct = place(step)
        block = hh * q + qq

        @pl.when((direct == 0) & (q + block != me))
        def _():
            to_reducer(step, block).wait_send()

        @pl.when(direct == 1)
        def _():
            for k in range(1, blocks):
                to_centre(step, j, k).wait_send()

        return carry

    lax.fori_loop(0, 2 * q, finish, 0)
    for kind in KINDS:
        for j in range(1 if kind == "plane" else 0, q):
            block_to(kind, j).wait_send()
    for at, kind in enumerate(("outer", "centre", "near")):
        val_to(at, kind).wait_send()
    for k in range(1, q):
        share(k).wait_send()

    @pl.when(is_outer)
    def _():
        scr_copy.wait_send()

    @pl.when(is_centre)
    def _():
        for k in range(1, blocks):
            early_copy(k).wait_send()
        for to in range(n):
            @pl.when(to != me)
            def _():
                field_copy_to(to).wait_send()


def project_kernel(condt_ref, valt_ref, field_ref, out_hbm, held, out_sem):
    v = valt_ref.shape[0]
    batch = field_ref.shape[0]
    valt = valt_ref[...]
    copies = []
    for b in range(0, batch, 4):
        weights = jnp.concatenate(
            [valt * field_ref[b + i:b + i + 1, :].astype(jnp.bfloat16) for i in range(4)], axis=0
        )
        summed = lax.dot_general(condt_ref[...], weights, NT, preferred_element_type=jnp.float32)
        for i in range(4):
            held[b + i] = summed[:, i * v:(i + 1) * v].astype(jnp.bfloat16)
        copy = pltpu.make_async_copy(held.at[pl.ds(b, 4)], out_hbm.at[pl.ds(b, 4)], out_sem.at[b // 4])
        copy.start()
        copies.append(copy)
    for copy in copies:
        copy.wait()


def fast_body(n, excitations, valence_orb, conduction_orb, screened):
    batch, cl, v = excitations.shape
    rows, points = screened.shape
    q, first_late = n // 4, 2
    blocks, lates = 2 * q, q - first_late
    bf, f32, sent_as = jnp.bfloat16, jnp.float32, jnp.bfloat16
    hbm = pl.BlockSpec(memory_space=pltpu.HBM)
    vmem = pl.BlockSpec(memory_space=pltpu.VMEM)
    dma = pltpu.SemaphoreType.DMA
    condt, valt, field = pl.pallas_call(
        functools.partial(gather_kernel, n, first_late),
        out_shape=(
            jax.ShapeDtypeStruct((cl, points), bf),
            jax.ShapeDtypeStruct((v, points), bf),
            jax.ShapeDtypeStruct((batch, points), f32),
        ),
        in_specs=[hbm, hbm, hbm, hbm],
        out_specs=(vmem, vmem, vmem),
        scratch_shapes=[
            pltpu.VMEM((batch, cl, v), bf),
            pltpu.VMEM((batch * v, cl), bf),
            pltpu.VMEM((n, rows, cl), bf),
            pltpu.VMEM((q, 4, rows, v), bf),
            pltpu.VMEM((2, rows, points), bf),
            pltpu.VMEM((points, 2 * rows), bf),
            pltpu.VMEM((blocks, batch, 2 * rows), sent_as),
            pltpu.VMEM((n, batch, 2 * rows), sent_as),
            pltpu.VMEM((batch, 2 * rows), f32),
            pltpu.VMEM((blocks, batch, 2 * rows), f32),
            pltpu.VMEM((blocks, lates, batch, 2 * rows), sent_as),
            pltpu.VMEM((batch, 2 * rows), bf),
            pltpu.VMEM((blocks, batch, 2 * rows), bf),
            dma, dma((2,)),
            dma((n,)), dma((n,)), dma, dma, dma((3,)), dma((4,)), dma((q,)), dma((q,)),
            dma((blocks,)), dma((n,)), dma((blocks,)), dma((blocks,)),
            dma((lates, blocks)), dma((blocks, lates)), dma((n,)), dma((blocks,)),
        ],
        compiler_params=pltpu.CompilerParams(
            collective_id=0, has_side_effects=True, vmem_limit_bytes=24 * 1024 * 1024
        ),
        name="gather_field",
    )(*[pltpu.with_memory_space_constraint(x, pltpu.HBM) for x in (excitations, valence_orb, conduction_orb, screened)])
    return pl.pallas_call(
        project_kernel,
        out_shape=jax.ShapeDtypeStruct((batch, cl, v), bf),
        in_specs=[vmem, vmem, vmem],
        out_specs=hbm,
        scratch_shapes=[pltpu.VMEM((batch, cl, v), bf), dma((batch // 4,))],
        compiler_params=pltpu.CompilerParams(vmem_limit_bytes=24 * 1024 * 1024),
        name="project",
    )(condt, valt, field)


def over_blocks(total_rows, step_fn, initial):
    span_size = math.gcd(total_rows, 2048)
    block_count = total_rows // span_size
    if block_count == 1:
        return step_fn(initial, 0, span_size)
    return lax.fori_loop(
        0, block_count, lambda index, carry: step_fn(carry, index * span_size, span_size), initial
    )


def density_rows(flat_exc, batch, valence_rows, cond_rows):
    total_rows = valence_rows.shape[0]
    cond_local = cond_rows.shape[1]
    initial = jnp.zeros((batch, total_rows), jnp.float32)

    def step_fn(carry, offset, span_size):
        val_block = lax.dynamic_slice_in_dim(valence_rows, offset, span_size, 0)
        cond_block = lax.dynamic_slice_in_dim(cond_rows, offset, span_size, 0)
        mixed = lax.dot_general(
            flat_exc, val_block, (((1,), (1,)), ((), ())), preferred_element_type=jnp.float32
        )
        mixed = mixed.reshape(batch, cond_local, span_size)
        summed = jnp.sum(mixed * cond_block.T.astype(jnp.float32)[None], axis=1)
        return lax.dynamic_update_slice_in_dim(carry, summed, offset, 1)

    return over_blocks(total_rows, step_fn, initial)


def projection(carry, valence_rows, cond_rows, field_cols):
    total_rows = valence_rows.shape[0]
    batch = field_cols.shape[0]
    cond_local = cond_rows.shape[1]

    def step_fn(inner, offset, span_size):
        val_block = lax.dynamic_slice_in_dim(valence_rows, offset, span_size, 0)
        cond_block = lax.dynamic_slice_in_dim(cond_rows, offset, span_size, 0)
        field_block = lax.dynamic_slice_in_dim(field_cols, offset, span_size, 1)
        pair = (
            cond_block.T.astype(jnp.float32)[None] * field_block.astype(jnp.float32)[:, None, :]
        ).astype(jnp.bfloat16)
        pair = pair.reshape(batch * cond_local, span_size)
        return inner + jnp.dot(pair, val_block, preferred_element_type=jnp.float32)

    return over_blocks(total_rows, step_fn, carry)


def general_body(excitations, valence_orb, conduction_orb, screened):
    batch, cond_local, valence = excitations.shape
    flat_exc = excitations.reshape(batch * cond_local, valence)
    valence_whole = lax.all_gather(valence_orb, "row", axis=0, tiled=True)
    cond_rows = lax.all_to_all(conduction_orb, "row", split_axis=1, concat_axis=0, tiled=True)
    partial_density = density_rows(flat_exc, batch, valence_whole, cond_rows)
    density_whole = lax.psum(partial_density, "row").astype(jnp.bfloat16)
    field_mine = lax.dot_general(
        density_whole, screened, (((1,), (1,)), ((), ())), preferred_element_type=jnp.float32
    ).astype(jnp.bfloat16)
    initial = jnp.zeros((batch * cond_local, valence), jnp.float32)
    summed = projection(
        initial, valence_whole, cond_rows, lax.all_gather(field_mine, "row", axis=1, tiled=True)
    )
    return summed.reshape(batch, cond_local, valence).astype(jnp.bfloat16)


def body(n, excitations, valence_orb, conduction_orb, screened):
    batch, cl, v = excitations.shape
    rows = valence_orb.shape[0]
    fits = n == 16 and cl % 128 == 0 and v == 128 and rows == 64 and batch == 16
    if fits:
        return fast_body(n, excitations, valence_orb, conduction_orb, screened)
    return general_body(excitations, valence_orb, conduction_orb, screened)


def solution(mesh):
    in_specs = (
        P("grp", "row", None),
        P(("grp", "row"), None),
        P(("grp", "row"), None),
        P(("grp", "row"), None),
    )
    out_specs = P("grp", "row", None)
    return jax.shard_map(
        functools.partial(body, mesh.shape["row"]),
        mesh=mesh, in_specs=in_specs, out_specs=out_specs, check_vma=False,
    )
```

```python
import functools
import math

import jax
import jax.numpy as jnp
from jax import lax
from jax.experimental import pallas as pl
from jax.experimental.pallas import tpu as pltpu
from jax.sharding import PartitionSpec as P

MESH = pl.DeviceIdType.MESH
NT = (((1,), (1,)), ((), ()))


def flip(index, other, bits):
    total = 0
    for bit in range(bits):
        a = (index // (1 << bit)) % 2
        b = (other // (1 << bit)) % 2
        total = total + (a + b - 2 * a * b) * (1 << bit)
    return total


KINDS = ("outer", "centre", "near", "plane")


def gather_kernel(
    n, first_late,
    exc_hbm, val_ref, cond_hbm, scr_ref,
    condt_ref, valt_ref, field_ref, exc, exct, cond_all, val_all, scr_pair, scr_mixed,
    part, tail, red, early, early_all, late, fld, fld_all,
    exc_sem, own_sem,
    cond_send, cond_recv, scr_send, scr_recv, va_send, va_recv, vb_send, vb_recv,
    part_send, red_recv, early_send, early_recv, late_send, late_recv, fld_send, fld_recv,
):
    rows, cl = val_ref.shape[0], exc.shape[1]
    batch = exc.shape[0]
    q = n // 4
    qbits, bits = q.bit_length() - 1, n.bit_length() - 1
    blocks, bbits = 2 * q, q.bit_length()
    me = lax.axis_index("row")
    my_z, my_q = me // q, me % q
    half = my_z // 2
    outer = (my_z + 1 + half) % 2
    is_outer, is_centre = outer == 1, outer == 0
    mine = half * q + my_q

    barrier = pltpu.get_barrier_semaphore()
    for k in range(n - 1, 0, -1):
        to = flip(me, k, bits)

        pl.semaphore_signal(barrier, inc=1, device_id={"row": to}, device_id_type=MESH)

    exc_copy = pltpu.make_async_copy(exc_hbm, exc, exc_sem)
    exc_copy.start()
    own_val = pltpu.make_async_copy(val_ref, val_all.at[my_q, my_z], own_sem.at[0])
    own_val.start()
    own_scr = pltpu.make_async_copy(scr_ref, scr_pair.at[my_z % 2], own_sem.at[1])
    own_scr.start()
    pltpu.make_async_copy(
        cond_hbm.at[:, pl.ds(pl.multiple_of(me * cl, cl), cl)], cond_all.at[me], cond_recv.at[me]
    ).start()
    pl.semaphore_wait(barrier, n - 1)

    def remote(src, dst, send, recv, to):
        return pltpu.make_async_remote_copy(
            src_ref=src, dst_ref=dst, send_sem=send, recv_sem=recv,
            device_id={"row": to}, device_id_type=MESH,
        )

    def device(kind, j):
        z = {"outer": 3 * (1 - half), "centre": 2 - half, "near": flip(my_z, 1, 2), "plane": my_z}[kind]
        return z * q + flip(my_q, j, qbits)

    def block_to(kind, j):
        to = device(kind, j)
        return remote(
            cond_hbm.at[:, pl.ds(pl.multiple_of(to * cl, cl), cl)], cond_all.at[me],
            cond_send.at[KINDS.index(kind) * q + j], cond_recv.at[me], to,
        )

    def val_to(at, kind):
        return remote(val_ref, val_all.at[my_q, my_z], va_send.at[at], va_recv.at[my_z], device(kind, 0))

    scr_copy = remote(scr_ref, scr_pair.at[my_z % 2], scr_send, scr_recv, device("near", 0))

    val_to(0, "outer").start()
    val_to(1, "centre").start()
    val_to(2, "near").start()
    for j in range(q):
        block_to("outer", j).start()


    exc_copy.wait()

    def turn(b, carry):
        exct[pl.ds(pl.multiple_of(b * 128, 128), 128), :] = exc[b].T
        return carry

    lax.fori_loop(0, batch, turn, 0)

    own_val.wait()
    def val_wait(z):
        pltpu.make_async_copy(val_ref, val_all.at[my_q, z], va_recv.at[z]).wait()

    def share(k):
        return remote(val_all.at[my_q], val_all.at[my_q], vb_send.at[k], vb_recv.at[my_q], device("plane", k))

    for k in range(1, 4):
        val_wait(flip(my_z, k, 2))
    for k in range(1, q):
        share(k).start()
    for j in range(1, q):
        block_to("plane", j).start()
    for j in range(q):
        block_to("near", j).start()

    @pl.when(is_centre)
    def _():
        for j in range(q):
            block_to("centre", j).start()

    @pl.when(is_outer)
    def _():
        scr_copy.start()

    for k in range(1, q):
        other = flip(my_q, k, qbits)
        pltpu.make_async_copy(val_all.at[other], val_all.at[other], vb_recv.at[other]).wait()

    def place(step):
        cross, j = (step // q + outer) % 2, step % q
        hh, qq = (half + cross) % 2, flip(my_q, j, qbits)
        direct = jnp.where((outer == 0) & (cross == 1) & (j >= first_late), 1, 0)
        return hh, qq, j, direct

    def to_reducer(step, block):
        return remote(part.at[step], red.at[me], part_send.at[step], red_recv.at[me], q + block)

    def to_centre(step, j, k):
        return remote(
            tail.at[j - first_late], late.at[mine, j - first_late], late_send.at[j - first_late, k],
            late_recv.at[mine, j - first_late], q + flip(mine, k, bbits),
        )

    def group(step, carry):
        hh, qq, j, direct = place(step)
        block = hh * q + qq
        lanes = pl.ds(pl.multiple_of(block * 2 * rows, 2 * rows), 2 * rows)
        first = 2 * hh * q + qq
        for i in range(2):
            pltpu.make_async_copy(
                cond_all.at[first + i * q], cond_all.at[first + i * q], cond_recv.at[first + i * q]
            ).wait()
        cond = jnp.concatenate([cond_all[first], cond_all[first + q]], axis=0)
        vals = val_all[qq, pl.ds(2 * hh, 2)].reshape(2 * rows, val_ref.shape[1])
        valt = vals.astype(jnp.float32).T
        valt_ref[:, lanes] = valt.astype(jnp.bfloat16)
        mixed = lax.dot_general(exct[...], cond, NT, preferred_element_type=jnp.float32)
        summed = jnp.sum(mixed.reshape(batch, valt.shape[0], 2 * rows) * valt[None], axis=1)
        part[step] = summed.astype(part.dtype)

        @pl.when((direct == 0) & (q + block != me))
        def _():
            to_reducer(step, block).start()

        @pl.when((direct == 0) & (q + block == me))
        def _():
            red[me] = summed.astype(red.dtype)

        @pl.when(direct == 1)
        def _():
            tail[j - first_late] = summed.astype(tail.dtype)
            for k in range(blocks - 1, 0, -1):
                to_centre(step, j, k).start()
            late[mine, j - first_late] = summed.astype(late.dtype)

        condt_ref[:, lanes] = cond.T

        @pl.when((outer == 1) & (step < q))
        def _():
            block_to("centre", step).start()

        return carry

    lax.fori_loop(0, q, group, 0)

    own_scr.wait()

    @pl.when(is_centre)
    def _():
        other = 1 - my_z % 2
        pltpu.make_async_copy(scr_pair.at[other], scr_pair.at[other], scr_recv).wait()
        whole = scr_pair[...].reshape(2 * rows, scr_ref.shape[1]).astype(jnp.float32)
        for h in range(2):
            for i in range(q):
                first = 2 * h * q + i
                pieces = [whole[:, d * rows:(d + 1) * rows] for d in (first, first + q)]
                at = (h * q + i) * 2 * rows
                scr_mixed[at:at + 2 * rows, :] = jnp.concatenate(pieces, axis=1).T.astype(jnp.bfloat16)

    lax.fori_loop(q, 2 * q - 1, group, 0)

    def early_copy(k):
        return remote(
            early, early_all.at[mine], early_send.at[k], early_recv.at[mine], q + flip(mine, k, bbits)
        )

    @pl.when(is_centre)
    def _():
        own_outer, own_centre = 3 * half * q, (1 + half) * q
        far_outer, far_centre = 3 * (1 - half) * q, (2 - half) * q
        total = red[me].astype(jnp.float32)
        others = [(own_outer, j) for j in range(q)] + [(own_centre, j) for j in range(1, q)]
        others += [(far_outer, j) for j in range(q)] + [(far_centre, j) for j in range(first_late)]
        for base, j in others:
            other = base + flip(my_q, j, qbits)
            pltpu.make_async_copy(red.at[other], red.at[other], red_recv.at[other]).wait()
            total = total + red[other].astype(jnp.float32)
        early[...] = total.astype(early.dtype)
        early_all[mine] = total.astype(early.dtype)
        for k in range(blocks - 1, 0, -1):
            early_copy(k).start()

    group(2 * q - 1, 0)

    def field_copy_to(k):
        return remote(fld, fld_all.at[mine], fld_send.at[k], fld_recv.at[mine], k)

    @pl.when(is_centre)
    def _():
        for k in range(1, blocks):
            other = flip(mine, k, bbits)
            pltpu.make_async_copy(early_all.at[other], early_all.at[other], early_recv.at[other]).wait()
        dens = [early_all[block].astype(jnp.float32) for block in range(blocks)]
        for j in range(first_late, q):
            at = j - first_late
            for k in range(1, blocks):
                other = flip(mine, k, bbits)
                pltpu.make_async_copy(late.at[other, at], late.at[other, at], late_recv.at[other, at]).wait()
            for block in range(blocks):
                source = (1 - block // q) * q + flip(block % q, j, qbits)
                dens[block] = dens[block] + late[source, at].astype(jnp.float32)
        whole = jnp.concatenate(dens, axis=1).astype(jnp.bfloat16)
        got = jnp.dot(whole, scr_mixed[...], preferred_element_type=jnp.float32).astype(jnp.bfloat16)
        fld[...] = got
        fld_all[mine] = got
        for to in [*range(q), *range(3 * q, n), *range(2 * q, 3 * q), *range(q, 2 * q)]:
            @pl.when(to != me)
            def _():
                field_copy_to(to).start()

    for k in range(1, blocks):
        other = flip(mine, k, bbits)
        pltpu.make_async_copy(fld_all.at[other], fld_all.at[other], fld_recv.at[other]).wait()

    @pl.when(is_outer)
    def _():
        pltpu.make_async_copy(fld_all.at[mine], fld_all.at[mine], fld_recv.at[mine]).wait()

    for block in range(blocks):
        field_ref[:, block * 2 * rows:(block + 1) * 2 * rows] = fld_all[block].astype(jnp.float32)

    def finish(step, carry):
        hh, qq, j, direct = place(step)
        block = hh * q + qq

        @pl.when((direct == 0) & (q + block != me))
        def _():
            to_reducer(step, block).wait_send()

        @pl.when(direct == 1)
        def _():
            for k in range(1, blocks):
                to_centre(step, j, k).wait_send()

        return carry

    lax.fori_loop(0, 2 * q, finish, 0)
    for kind in KINDS:
        for j in range(1 if kind == "plane" else 0, q):
            block_to(kind, j).wait_send()
    for at, kind in enumerate(("outer", "centre", "near")):
        val_to(at, kind).wait_send()
    for k in range(1, q):
        share(k).wait_send()

    @pl.when(is_outer)
    def _():
        scr_copy.wait_send()

    @pl.when(is_centre)
    def _():
        for k in range(1, blocks):
            early_copy(k).wait_send()
        for to in range(n):
            @pl.when(to != me)
            def _():
                field_copy_to(to).wait_send()


def project_kernel(condt_ref, valt_ref, field_ref, out_hbm, held, out_sem):
    v = valt_ref.shape[0]
    batch = field_ref.shape[0]
    valt = valt_ref[...]
    copies = []
    for b in range(0, batch, 4):
        weights = jnp.concatenate(
            [valt * field_ref[b + i:b + i + 1, :].astype(jnp.bfloat16) for i in range(4)], axis=0
        )
        summed = lax.dot_general(condt_ref[...], weights, NT, preferred_element_type=jnp.float32)
        for i in range(4):
            held[b + i] = summed[:, i * v:(i + 1) * v].astype(jnp.bfloat16)
        copy = pltpu.make_async_copy(held.at[pl.ds(b, 4)], out_hbm.at[pl.ds(b, 4)], out_sem.at[b // 4])
        copy.start()
        copies.append(copy)
    for copy in copies:
        copy.wait()


def fast_body(n, excitations, valence_orb, conduction_orb, screened):
    batch, cl, v = excitations.shape
    rows, points = screened.shape
    q, first_late = n // 4, 2
    blocks, lates = 2 * q, q - first_late
    bf, f32 = jnp.bfloat16, jnp.float32
    hbm = pl.BlockSpec(memory_space=pltpu.HBM)
    vmem = pl.BlockSpec(memory_space=pltpu.VMEM)
    dma = pltpu.SemaphoreType.DMA
    condt, valt, field = pl.pallas_call(
        functools.partial(gather_kernel, n, first_late),
        out_shape=(
            jax.ShapeDtypeStruct((cl, points), bf),
            jax.ShapeDtypeStruct((v, points), bf),
            jax.ShapeDtypeStruct((batch, points), f32),
        ),
        in_specs=[hbm, hbm, hbm, hbm],
        out_specs=(vmem, vmem, vmem),
        scratch_shapes=[
            pltpu.VMEM((batch, cl, v), bf),
            pltpu.VMEM((batch * v, cl), bf),
            pltpu.VMEM((n, rows, cl), bf),
            pltpu.VMEM((q, 4, rows, v), bf),
            pltpu.VMEM((2, rows, points), bf),
            pltpu.VMEM((points, 2 * rows), bf),
            pltpu.VMEM((blocks, batch, 2 * rows), bf),
            pltpu.VMEM((lates, batch, 2 * rows), f32),
            pltpu.VMEM((n, batch, 2 * rows), bf),
            pltpu.VMEM((batch, 2 * rows), f32),
            pltpu.VMEM((blocks, batch, 2 * rows), f32),
            pltpu.VMEM((blocks, lates, batch, 2 * rows), f32),
            pltpu.VMEM((batch, 2 * rows), bf),
            pltpu.VMEM((blocks, batch, 2 * rows), bf),
            dma, dma((2,)),
            dma((n,)), dma((n,)), dma, dma, dma((3,)), dma((4,)), dma((q,)), dma((q,)),
            dma((blocks,)), dma((n,)), dma((blocks,)), dma((blocks,)),
            dma((lates, blocks)), dma((blocks, lates)), dma((n,)), dma((blocks,)),
        ],
        compiler_params=pltpu.CompilerParams(
            collective_id=0, has_side_effects=True, vmem_limit_bytes=24 * 1024 * 1024
        ),
        name="gather_field",
    )(*[pltpu.with_memory_space_constraint(x, pltpu.HBM) for x in (excitations, valence_orb, conduction_orb, screened)])
    return pl.pallas_call(
        project_kernel,
        out_shape=jax.ShapeDtypeStruct((batch, cl, v), bf),
        in_specs=[vmem, vmem, vmem],
        out_specs=hbm,
        scratch_shapes=[pltpu.VMEM((batch, cl, v), bf), dma((batch // 4,))],
        compiler_params=pltpu.CompilerParams(vmem_limit_bytes=24 * 1024 * 1024),
        name="project",
    )(condt, valt, field)


def over_blocks(total_rows, step_fn, initial):
    span_size = math.gcd(total_rows, 2048)
    block_count = total_rows // span_size
    if block_count == 1:
        return step_fn(initial, 0, span_size)
    return lax.fori_loop(
        0, block_count, lambda index, carry: step_fn(carry, index * span_size, span_size), initial
    )


def density_rows(flat_exc, batch, valence_rows, cond_rows):
    total_rows = valence_rows.shape[0]
    cond_local = cond_rows.shape[1]
    initial = jnp.zeros((batch, total_rows), jnp.float32)

    def step_fn(carry, offset, span_size):
        val_block = lax.dynamic_slice_in_dim(valence_rows, offset, span_size, 0)
        cond_block = lax.dynamic_slice_in_dim(cond_rows, offset, span_size, 0)
        mixed = lax.dot_general(
            flat_exc, val_block, (((1,), (1,)), ((), ())), preferred_element_type=jnp.float32
        )
        mixed = mixed.reshape(batch, cond_local, span_size)
        summed = jnp.sum(mixed * cond_block.T.astype(jnp.float32)[None], axis=1)
        return lax.dynamic_update_slice_in_dim(carry, summed, offset, 1)

    return over_blocks(total_rows, step_fn, initial)


def projection(carry, valence_rows, cond_rows, field_cols):
    total_rows = valence_rows.shape[0]
    batch = field_cols.shape[0]
    cond_local = cond_rows.shape[1]

    def step_fn(inner, offset, span_size):
        val_block = lax.dynamic_slice_in_dim(valence_rows, offset, span_size, 0)
        cond_block = lax.dynamic_slice_in_dim(cond_rows, offset, span_size, 0)
        field_block = lax.dynamic_slice_in_dim(field_cols, offset, span_size, 1)
        pair = (
            cond_block.T.astype(jnp.float32)[None] * field_block.astype(jnp.float32)[:, None, :]
        ).astype(jnp.bfloat16)
        pair = pair.reshape(batch * cond_local, span_size)
        return inner + jnp.dot(pair, val_block, preferred_element_type=jnp.float32)

    return over_blocks(total_rows, step_fn, carry)


def general_body(excitations, valence_orb, conduction_orb, screened):
    batch, cond_local, valence = excitations.shape
    flat_exc = excitations.reshape(batch * cond_local, valence)
    valence_whole = lax.all_gather(valence_orb, "row", axis=0, tiled=True)
    cond_rows = lax.all_to_all(conduction_orb, "row", split_axis=1, concat_axis=0, tiled=True)
    partial_density = density_rows(flat_exc, batch, valence_whole, cond_rows)
    density_whole = lax.psum(partial_density, "row").astype(jnp.bfloat16)
    field_mine = lax.dot_general(
        density_whole, screened, (((1,), (1,)), ((), ())), preferred_element_type=jnp.float32
    ).astype(jnp.bfloat16)
    initial = jnp.zeros((batch * cond_local, valence), jnp.float32)
    summed = projection(
        initial, valence_whole, cond_rows, lax.all_gather(field_mine, "row", axis=1, tiled=True)
    )
    return summed.reshape(batch, cond_local, valence).astype(jnp.bfloat16)


def body(n, excitations, valence_orb, conduction_orb, screened):
    batch, cl, v = excitations.shape
    rows = valence_orb.shape[0]
    fits = n == 16 and cl % 128 == 0 and v == 128 and rows == 64 and batch == 16
    if fits:
        return fast_body(n, excitations, valence_orb, conduction_orb, screened)
    return general_body(excitations, valence_orb, conduction_orb, screened)


def solution(mesh):
    in_specs = (
        P("grp", "row", None),
        P(("grp", "row"), None),
        P(("grp", "row"), None),
        P(("grp", "row"), None),
    )
    out_specs = P("grp", "row", None)
    return jax.shard_map(
        functools.partial(body, mesh.shape["row"]),
        mesh=mesh, in_specs=in_specs, out_specs=out_specs, check_vma=False,
    )
```

```python
import functools
import math

import jax
import jax.numpy as jnp
from jax import lax
from jax.experimental import pallas as pl
from jax.experimental.pallas import tpu as pltpu
from jax.sharding import PartitionSpec as P

MESH = pl.DeviceIdType.MESH
NT = (((1,), (1,)), ((), ()))


def flip(index, other, bits):
    total = 0
    for bit in range(bits):
        a = (index // (1 << bit)) % 2
        b = (other // (1 << bit)) % 2
        total = total + (a + b - 2 * a * b) * (1 << bit)
    return total


KINDS = ("outer", "centre", "near", "plane")


def gather_kernel(
    n, first_late,
    exc_hbm, val_ref, cond_hbm, scr_ref,
    condt_ref, valt_ref, field_ref, exc, exct, cond_all, val_all, scr_pair, scr_mixed,
    part, red, early, early_all, late, fld, fld_all,
    exc_sem, own_sem,
    cond_send, cond_recv, scr_send, scr_recv, va_send, va_recv, vb_send, vb_recv,
    part_send, red_recv, early_send, early_recv, late_send, late_recv, fld_send, fld_recv,
):
    rows, cl = val_ref.shape[0], exc.shape[1]
    batch = exc.shape[0]
    q = n // 4
    qbits, bits = q.bit_length() - 1, n.bit_length() - 1
    blocks, bbits = 2 * q, q.bit_length()
    me = lax.axis_index("row")
    my_z, my_q = me // q, me % q
    half = my_z // 2
    outer = (my_z + 1 + half) % 2
    is_outer, is_centre = outer == 1, outer == 0
    mine = half * q + my_q

    barrier = pltpu.get_barrier_semaphore()
    for k in range(n - 1, 0, -1):
        to = flip(me, k, bits)

        pl.semaphore_signal(barrier, inc=1, device_id={"row": to}, device_id_type=MESH)

    exc_copy = pltpu.make_async_copy(exc_hbm, exc, exc_sem)
    exc_copy.start()
    own_val = pltpu.make_async_copy(val_ref, val_all.at[my_q, my_z], own_sem.at[0])
    own_val.start()
    own_scr = pltpu.make_async_copy(scr_ref, scr_pair.at[my_z % 2], own_sem.at[1])
    own_scr.start()
    pltpu.make_async_copy(
        cond_hbm.at[:, pl.ds(pl.multiple_of(me * cl, cl), cl)], cond_all.at[me], cond_recv.at[me]
    ).start()
    pl.semaphore_wait(barrier, n - 1)

    def remote(src, dst, send, recv, to):
        return pltpu.make_async_remote_copy(
            src_ref=src, dst_ref=dst, send_sem=send, recv_sem=recv,
            device_id={"row": to}, device_id_type=MESH,
        )

    def device(kind, j):
        z = {"outer": 3 * (1 - half), "centre": 2 - half, "near": flip(my_z, 1, 2), "plane": my_z}[kind]
        return z * q + flip(my_q, j, qbits)

    def block_to(kind, j):
        to = device(kind, j)
        return remote(
            cond_hbm.at[:, pl.ds(pl.multiple_of(to * cl, cl), cl)], cond_all.at[me],
            cond_send.at[KINDS.index(kind) * q + j], cond_recv.at[me], to,
        )

    def val_to(at, kind):
        return remote(val_ref, val_all.at[my_q, my_z], va_send.at[at], va_recv.at[my_z], device(kind, 0))

    scr_copy = remote(scr_ref, scr_pair.at[my_z % 2], scr_send, scr_recv, device("near", 0))

    val_to(0, "outer").start()
    val_to(1, "centre").start()
    val_to(2, "near").start()
    block_to("outer", 0).start()


    exc_copy.wait()

    def turn(b, carry):
        exct[pl.ds(pl.multiple_of(b * 128, 128), 128), :] = exc[b].T
        return carry

    lax.fori_loop(0, batch, turn, 0)

    own_val.wait()
    def val_wait(z):
        pltpu.make_async_copy(val_ref, val_all.at[my_q, z], va_recv.at[z]).wait()

    def share(k):
        return remote(val_all.at[my_q], val_all.at[my_q], vb_send.at[k], vb_recv.at[my_q], device("plane", k))

    for k in range(1, 4):
        val_wait(flip(my_z, k, 2))
    for k in range(1, q):
        share(k).start()
    for j in range(1, q):
        block_to("outer", j).start()
    for j in range(1, q):
        block_to("plane", j).start()
    for j in range(q):
        block_to("near", j).start()

    @pl.when(is_centre)
    def _():
        for j in range(q):
            block_to("centre", j).start()

    @pl.when(is_outer)
    def _():
        scr_copy.start()

    for k in range(1, q):
        other = flip(my_q, k, qbits)
        pltpu.make_async_copy(val_all.at[other], val_all.at[other], vb_recv.at[other]).wait()

    def place(step):
        cross, j = (step // q + outer) % 2, step % q
        hh, qq = (half + cross) % 2, flip(my_q, j, qbits)
        direct = jnp.where((outer == 0) & (cross == 1) & (j >= first_late), 1, 0)
        return hh, qq, j, direct

    def to_reducer(step, block):
        return remote(part.at[step], red.at[me], part_send.at[step], red_recv.at[me], q + block)

    def to_centre(step, j, k):
        return remote(
            part.at[step], late.at[mine, j - first_late], late_send.at[j - first_late, k],
            late_recv.at[mine, j - first_late], q + flip(mine, k, bbits),
        )

    def group(step, carry):
        hh, qq, j, direct = place(step)
        block = hh * q + qq
        lanes = pl.ds(pl.multiple_of(block * 2 * rows, 2 * rows), 2 * rows)
        first = 2 * hh * q + qq
        for i in range(2):
            pltpu.make_async_copy(
                cond_all.at[first + i * q], cond_all.at[first + i * q], cond_recv.at[first + i * q]
            ).wait()
        cond = jnp.concatenate([cond_all[first], cond_all[first + q]], axis=0)
        vals = val_all[qq, pl.ds(2 * hh, 2)].reshape(2 * rows, val_ref.shape[1])
        valt = vals.astype(jnp.float32).T
        valt_ref[:, lanes] = valt.astype(jnp.bfloat16)
        mixed = lax.dot_general(exct[...], cond, NT, preferred_element_type=jnp.float32)
        summed = jnp.sum(mixed.reshape(batch, valt.shape[0], 2 * rows) * valt[None], axis=1)
        part[step] = summed.astype(part.dtype)

        @pl.when((direct == 0) & (q + block != me))
        def _():
            to_reducer(step, block).start()

        @pl.when((direct == 0) & (q + block == me))
        def _():
            red[me] = summed.astype(red.dtype)

        @pl.when(direct == 1)
        def _():
            for k in range(blocks - 1, 0, -1):
                to_centre(step, j, k).start()
            late[mine, j - first_late] = summed.astype(late.dtype)

        condt_ref[:, lanes] = cond.T

        @pl.when((outer == 1) & (step < q))
        def _():
            block_to("centre", step).start()

        return carry

    lax.fori_loop(0, q, group, 0)

    own_scr.wait()

    @pl.when(is_centre)
    def _():
        other = 1 - my_z % 2
        pltpu.make_async_copy(scr_pair.at[other], scr_pair.at[other], scr_recv).wait()
        whole = scr_pair[...].reshape(2 * rows, scr_ref.shape[1]).astype(jnp.float32)
        for h in range(2):
            for i in range(q):
                first = 2 * h * q + i
                pieces = [whole[:, d * rows:(d + 1) * rows] for d in (first, first + q)]
                at = (h * q + i) * 2 * rows
                scr_mixed[at:at + 2 * rows, :] = jnp.concatenate(pieces, axis=1).T.astype(jnp.bfloat16)

    lax.fori_loop(q, 2 * q - 1, group, 0)

    def early_copy(k):
        return remote(
            early, early_all.at[mine], early_send.at[k], early_recv.at[mine], q + flip(mine, k, bbits)
        )

    @pl.when(is_centre)
    def _():
        own_outer, own_centre = 3 * half * q, (1 + half) * q
        far_outer, far_centre = 3 * (1 - half) * q, (2 - half) * q
        total = red[me].astype(jnp.float32)
        others = [(own_outer, j) for j in range(q)] + [(own_centre, j) for j in range(1, q)]
        others += [(far_outer, j) for j in range(q)] + [(far_centre, j) for j in range(first_late)]
        for base, j in others:
            other = base + flip(my_q, j, qbits)
            pltpu.make_async_copy(red.at[other], red.at[other], red_recv.at[other]).wait()
            total = total + red[other].astype(jnp.float32)
        early[...] = total.astype(early.dtype)
        early_all[mine] = total.astype(early.dtype)
        for k in range(blocks - 1, 0, -1):
            early_copy(k).start()

    group(2 * q - 1, 0)

    def field_copy_to(k):
        return remote(fld, fld_all.at[mine], fld_send.at[k], fld_recv.at[mine], k)

    @pl.when(is_centre)
    def _():
        for k in range(1, blocks):
            other = flip(mine, k, bbits)
            pltpu.make_async_copy(early_all.at[other], early_all.at[other], early_recv.at[other]).wait()
        dens = [early_all[block].astype(jnp.float32) for block in range(blocks)]
        for j in range(first_late, q):
            at = j - first_late
            for k in range(1, blocks):
                other = flip(mine, k, bbits)
                pltpu.make_async_copy(late.at[other, at], late.at[other, at], late_recv.at[other, at]).wait()
            for block in range(blocks):
                source = (1 - block // q) * q + flip(block % q, j, qbits)
                dens[block] = dens[block] + late[source, at].astype(jnp.float32)
        whole = jnp.concatenate(dens, axis=1).astype(jnp.bfloat16)
        got = jnp.dot(whole, scr_mixed[...], preferred_element_type=jnp.float32).astype(jnp.bfloat16)
        fld[...] = got
        fld_all[mine] = got
        for to in [*range(q), *range(3 * q, n), *range(2 * q, 3 * q), *range(q, 2 * q)]:
            @pl.when(to != me)
            def _():
                field_copy_to(to).start()

    for k in range(1, blocks):
        other = flip(mine, k, bbits)
        pltpu.make_async_copy(fld_all.at[other], fld_all.at[other], fld_recv.at[other]).wait()

    @pl.when(is_outer)
    def _():
        pltpu.make_async_copy(fld_all.at[mine], fld_all.at[mine], fld_recv.at[mine]).wait()

    for block in range(blocks):
        field_ref[:, block * 2 * rows:(block + 1) * 2 * rows] = fld_all[block].astype(jnp.float32)

    def finish(step, carry):
        hh, qq, j, direct = place(step)
        block = hh * q + qq

        @pl.when((direct == 0) & (q + block != me))
        def _():
            to_reducer(step, block).wait_send()

        @pl.when(direct == 1)
        def _():
            for k in range(1, blocks):
                to_centre(step, j, k).wait_send()

        return carry

    lax.fori_loop(0, 2 * q, finish, 0)
    for kind in KINDS:
        for j in range(1 if kind == "plane" else 0, q):
            block_to(kind, j).wait_send()
    for at, kind in enumerate(("outer", "centre", "near")):
        val_to(at, kind).wait_send()
    for k in range(1, q):
        share(k).wait_send()

    @pl.when(is_outer)
    def _():
        scr_copy.wait_send()

    @pl.when(is_centre)
    def _():
        for k in range(1, blocks):
            early_copy(k).wait_send()
        for to in range(n):
            @pl.when(to != me)
            def _():
                field_copy_to(to).wait_send()


def project_kernel(condt_ref, valt_ref, field_ref, out_hbm, held, out_sem):
    v = valt_ref.shape[0]
    batch = field_ref.shape[0]
    valt = valt_ref[...]
    copies = []
    for b in range(0, batch, 4):
        weights = jnp.concatenate(
            [valt * field_ref[b + i:b + i + 1, :].astype(jnp.bfloat16) for i in range(4)], axis=0
        )
        summed = lax.dot_general(condt_ref[...], weights, NT, preferred_element_type=jnp.float32)
        for i in range(4):
            held[b + i] = summed[:, i * v:(i + 1) * v].astype(jnp.bfloat16)
        copy = pltpu.make_async_copy(held.at[pl.ds(b, 4)], out_hbm.at[pl.ds(b, 4)], out_sem.at[b // 4])
        copy.start()
        copies.append(copy)
    for copy in copies:
        copy.wait()


def fast_body(n, excitations, valence_orb, conduction_orb, screened):
    batch, cl, v = excitations.shape
    rows, points = screened.shape
    q, first_late = n // 4, 2
    blocks, lates = 2 * q, q - first_late
    bf, f32, sent_as = jnp.bfloat16, jnp.float32, jnp.bfloat16
    hbm = pl.BlockSpec(memory_space=pltpu.HBM)
    vmem = pl.BlockSpec(memory_space=pltpu.VMEM)
    dma = pltpu.SemaphoreType.DMA
    condt, valt, field = pl.pallas_call(
        functools.partial(gather_kernel, n, first_late),
        out_shape=(
            jax.ShapeDtypeStruct((cl, points), bf),
            jax.ShapeDtypeStruct((v, points), bf),
            jax.ShapeDtypeStruct((batch, points), f32),
        ),
        in_specs=[hbm, hbm, hbm, hbm],
        out_specs=(vmem, vmem, vmem),
        scratch_shapes=[
            pltpu.VMEM((batch, cl, v), bf),
            pltpu.VMEM((batch * v, cl), bf),
            pltpu.VMEM((n, rows, cl), bf),
            pltpu.VMEM((q, 4, rows, v), bf),
            pltpu.VMEM((2, rows, points), bf),
            pltpu.VMEM((points, 2 * rows), bf),
            pltpu.VMEM((blocks, batch, 2 * rows), sent_as),
            pltpu.VMEM((n, batch, 2 * rows), sent_as),
            pltpu.VMEM((batch, 2 * rows), f32),
            pltpu.VMEM((blocks, batch, 2 * rows), f32),
            pltpu.VMEM((blocks, lates, batch, 2 * rows), sent_as),
            pltpu.VMEM((batch, 2 * rows), bf),
            pltpu.VMEM((blocks, batch, 2 * rows), bf),
            dma, dma((2,)),
            dma((n,)), dma((n,)), dma, dma, dma((3,)), dma((4,)), dma((q,)), dma((q,)),
            dma((blocks,)), dma((n,)), dma((blocks,)), dma((blocks,)),
            dma((lates, blocks)), dma((blocks, lates)), dma((n,)), dma((blocks,)),
        ],
        compiler_params=pltpu.CompilerParams(
            collective_id=0, has_side_effects=True, vmem_limit_bytes=24 * 1024 * 1024
        ),
        name="gather_field",
    )(*[pltpu.with_memory_space_constraint(x, pltpu.HBM) for x in (excitations, valence_orb, conduction_orb, screened)])
    return pl.pallas_call(
        project_kernel,
        out_shape=jax.ShapeDtypeStruct((batch, cl, v), bf),
        in_specs=[vmem, vmem, vmem],
        out_specs=hbm,
        scratch_shapes=[pltpu.VMEM((batch, cl, v), bf), dma((batch // 4,))],
        compiler_params=pltpu.CompilerParams(vmem_limit_bytes=24 * 1024 * 1024),
        name="project",
    )(condt, valt, field)


def over_blocks(total_rows, step_fn, initial):
    span_size = math.gcd(total_rows, 2048)
    block_count = total_rows // span_size
    if block_count == 1:
        return step_fn(initial, 0, span_size)
    return lax.fori_loop(
        0, block_count, lambda index, carry: step_fn(carry, index * span_size, span_size), initial
    )


def density_rows(flat_exc, batch, valence_rows, cond_rows):
    total_rows = valence_rows.shape[0]
    cond_local = cond_rows.shape[1]
    initial = jnp.zeros((batch, total_rows), jnp.float32)

    def step_fn(carry, offset, span_size):
        val_block = lax.dynamic_slice_in_dim(valence_rows, offset, span_size, 0)
        cond_block = lax.dynamic_slice_in_dim(cond_rows, offset, span_size, 0)
        mixed = lax.dot_general(
            flat_exc, val_block, (((1,), (1,)), ((), ())), preferred_element_type=jnp.float32
        )
        mixed = mixed.reshape(batch, cond_local, span_size)
        summed = jnp.sum(mixed * cond_block.T.astype(jnp.float32)[None], axis=1)
        return lax.dynamic_update_slice_in_dim(carry, summed, offset, 1)

    return over_blocks(total_rows, step_fn, initial)


def projection(carry, valence_rows, cond_rows, field_cols):
    total_rows = valence_rows.shape[0]
    batch = field_cols.shape[0]
    cond_local = cond_rows.shape[1]

    def step_fn(inner, offset, span_size):
        val_block = lax.dynamic_slice_in_dim(valence_rows, offset, span_size, 0)
        cond_block = lax.dynamic_slice_in_dim(cond_rows, offset, span_size, 0)
        field_block = lax.dynamic_slice_in_dim(field_cols, offset, span_size, 1)
        pair = (
            cond_block.T.astype(jnp.float32)[None] * field_block.astype(jnp.float32)[:, None, :]
        ).astype(jnp.bfloat16)
        pair = pair.reshape(batch * cond_local, span_size)
        return inner + jnp.dot(pair, val_block, preferred_element_type=jnp.float32)

    return over_blocks(total_rows, step_fn, carry)


def general_body(excitations, valence_orb, conduction_orb, screened):
    batch, cond_local, valence = excitations.shape
    flat_exc = excitations.reshape(batch * cond_local, valence)
    valence_whole = lax.all_gather(valence_orb, "row", axis=0, tiled=True)
    cond_rows = lax.all_to_all(conduction_orb, "row", split_axis=1, concat_axis=0, tiled=True)
    partial_density = density_rows(flat_exc, batch, valence_whole, cond_rows)
    density_whole = lax.psum(partial_density, "row").astype(jnp.bfloat16)
    field_mine = lax.dot_general(
        density_whole, screened, (((1,), (1,)), ((), ())), preferred_element_type=jnp.float32
    ).astype(jnp.bfloat16)
    initial = jnp.zeros((batch * cond_local, valence), jnp.float32)
    summed = projection(
        initial, valence_whole, cond_rows, lax.all_gather(field_mine, "row", axis=1, tiled=True)
    )
    return summed.reshape(batch, cond_local, valence).astype(jnp.bfloat16)


def body(n, excitations, valence_orb, conduction_orb, screened):
    batch, cl, v = excitations.shape
    rows = valence_orb.shape[0]
    fits = n == 16 and cl % 128 == 0 and v == 128 and rows == 64 and batch == 16
    if fits:
        return fast_body(n, excitations, valence_orb, conduction_orb, screened)
    return general_body(excitations, valence_orb, conduction_orb, screened)


def solution(mesh):
    in_specs = (
        P("grp", "row", None),
        P(("grp", "row"), None),
        P(("grp", "row"), None),
        P(("grp", "row"), None),
    )
    out_specs = P("grp", "row", None)
    return jax.shard_map(
        functools.partial(body, mesh.shape["row"]),
        mesh=mesh, in_specs=in_specs, out_specs=out_specs, check_vma=False,
    )
```

```python
import functools
import math

import jax
import jax.numpy as jnp
from jax import lax
from jax.experimental import pallas as pl
from jax.experimental.pallas import tpu as pltpu
from jax.sharding import PartitionSpec as P

MESH = pl.DeviceIdType.MESH
NT = (((1,), (1,)), ((), ()))


def flip(index, other, bits):
    total = 0
    for bit in range(bits):
        a = (index // (1 << bit)) % 2
        b = (other // (1 << bit)) % 2
        total = total + (a + b - 2 * a * b) * (1 << bit)
    return total


KINDS = ("outer", "centre", "near", "plane")


def gather_kernel(
    n, first_late,
    exc_hbm, val_ref, cond_hbm, scr_ref,
    condt_ref, valt_ref, field_ref, exc, exct, cond_all, val_all, scr_pair, scr_mixed,
    part, red, early, early_all, late, fld, fld_all,
    exc_sem, own_sem,
    cond_send, cond_recv, scr_send, scr_recv, va_send, va_recv, vb_send, vb_recv,
    part_send, red_recv, early_send, early_recv, late_send, late_recv, fld_send, fld_recv,
):
    rows, cl = val_ref.shape[0], exc.shape[1]
    batch = exc.shape[0]
    q = n // 4
    qbits, bits = q.bit_length() - 1, n.bit_length() - 1
    blocks, bbits = 2 * q, q.bit_length()
    me = lax.axis_index("row")
    my_z, my_q = me // q, me % q
    half = my_z // 2
    outer = (my_z + 1 + half) % 2
    is_outer, is_centre = outer == 1, outer == 0
    mine = half * q + my_q

    barrier = pltpu.get_barrier_semaphore()
    for k in [z * q + i for z in (2, 3, 1, 0) for i in range(q) if z or i]:
        to = flip(me, k, bits)

        pl.semaphore_signal(barrier, inc=1, device_id={"row": to}, device_id_type=MESH)

    exc_copy = pltpu.make_async_copy(exc_hbm, exc, exc_sem)
    exc_copy.start()
    own_val = pltpu.make_async_copy(val_ref, val_all.at[my_q, my_z], own_sem.at[0])
    own_val.start()
    own_scr = pltpu.make_async_copy(scr_ref, scr_pair.at[my_z % 2], own_sem.at[1])
    own_scr.start()
    pltpu.make_async_copy(
        cond_hbm.at[:, pl.ds(pl.multiple_of(me * cl, cl), cl)], cond_all.at[me], cond_recv.at[me]
    ).start()
    pl.semaphore_wait(barrier, n - 1)

    def remote(src, dst, send, recv, to):
        return pltpu.make_async_remote_copy(
            src_ref=src, dst_ref=dst, send_sem=send, recv_sem=recv,
            device_id={"row": to}, device_id_type=MESH,
        )

    def device(kind, j):
        z = {"outer": 3 * (1 - half), "centre": 2 - half, "near": flip(my_z, 1, 2), "plane": my_z}[kind]
        return z * q + flip(my_q, j, qbits)

    def block_to(kind, j):
        to = device(kind, j)
        return remote(
            cond_hbm.at[:, pl.ds(pl.multiple_of(to * cl, cl), cl)], cond_all.at[me],
            cond_send.at[KINDS.index(kind) * q + j], cond_recv.at[me], to,
        )

    def val_to(at, kind):
        return remote(val_ref, val_all.at[my_q, my_z], va_send.at[at], va_recv.at[my_z], device(kind, 0))

    scr_copy = remote(scr_ref, scr_pair.at[my_z % 2], scr_send, scr_recv, device("near", 0))

    val_to(0, "outer").start()
    val_to(1, "centre").start()
    val_to(2, "near").start()
    block_to("outer", 0).start()


    exc_copy.wait()

    def turn(b, carry):
        exct[pl.ds(pl.multiple_of(b * 128, 128), 128), :] = exc[b].T
        return carry

    lax.fori_loop(0, batch, turn, 0)

    own_val.wait()
    def val_wait(z):
        pltpu.make_async_copy(val_ref, val_all.at[my_q, z], va_recv.at[z]).wait()

    def share(k):
        return remote(val_all.at[my_q], val_all.at[my_q], vb_send.at[k], vb_recv.at[my_q], device("plane", k))

    for k in range(1, 4):
        val_wait(flip(my_z, k, 2))
    for k in range(1, q):
        share(k).start()
    for j in range(1, q):
        block_to("outer", j).start()
    for j in range(1, q):
        block_to("plane", j).start()
    for j in range(q):
        block_to("near", j).start()

    @pl.when(is_centre)
    def _():
        for j in range(q):
            block_to("centre", j).start()

    @pl.when(is_outer)
    def _():
        scr_copy.start()

    for k in range(1, q):
        other = flip(my_q, k, qbits)
        pltpu.make_async_copy(val_all.at[other], val_all.at[other], vb_recv.at[other]).wait()

    def place(step):
        cross, j = (step // q + outer) % 2, step % q
        hh, qq = (half + cross) % 2, flip(my_q, j, qbits)
        direct = jnp.where((outer == 0) & (cross == 1) & (j >= first_late), 1, 0)
        return hh, qq, j, direct

    def to_reducer(step, block):
        return remote(part.at[step], red.at[me], part_send.at[step], red_recv.at[me], q + block)

    def to_centre(step, j, k):
        return remote(
            part.at[step], late.at[mine, j - first_late], late_send.at[j - first_late, k],
            late_recv.at[mine, j - first_late], q + flip(mine, k, bbits),
        )

    def group(step, carry):
        hh, qq, j, direct = place(step)
        block = hh * q + qq
        lanes = pl.ds(pl.multiple_of(block * 2 * rows, 2 * rows), 2 * rows)
        first = 2 * hh * q + qq
        for i in range(2):
            pltpu.make_async_copy(
                cond_all.at[first + i * q], cond_all.at[first + i * q], cond_recv.at[first + i * q]
            ).wait()
        cond = jnp.concatenate([cond_all[first], cond_all[first + q]], axis=0)
        vals = val_all[qq, pl.ds(2 * hh, 2)].reshape(2 * rows, val_ref.shape[1])
        valt = vals.astype(jnp.float32).T
        valt_ref[:, lanes] = valt.astype(jnp.bfloat16)
        mixed = lax.dot_general(exct[...], cond, NT, preferred_element_type=jnp.float32)
        summed = jnp.sum(mixed.reshape(batch, valt.shape[0], 2 * rows) * valt[None], axis=1)
        part[step] = summed.astype(part.dtype)

        @pl.when((direct == 0) & (q + block != me))
        def _():
            to_reducer(step, block).start()

        @pl.when((direct == 0) & (q + block == me))
        def _():
            red[me] = summed.astype(red.dtype)

        @pl.when(direct == 1)
        def _():
            for k in range(blocks - 1, 0, -1):
                to_centre(step, j, k).start()
            late[mine, j - first_late] = summed.astype(late.dtype)

        condt_ref[:, lanes] = cond.T

        @pl.when((outer == 1) & (step < q))
        def _():
            block_to("centre", step).start()

        return carry

    lax.fori_loop(0, q, group, 0)

    own_scr.wait()

    @pl.when(is_centre)
    def _():
        other = 1 - my_z % 2
        pltpu.make_async_copy(scr_pair.at[other], scr_pair.at[other], scr_recv).wait()
        whole = scr_pair[...].reshape(2 * rows, scr_ref.shape[1]).astype(jnp.float32)
        for h in range(2):
            for i in range(q):
                first = 2 * h * q + i
                pieces = [whole[:, d * rows:(d + 1) * rows] for d in (first, first + q)]
                at = (h * q + i) * 2 * rows
                scr_mixed[at:at + 2 * rows, :] = jnp.concatenate(pieces, axis=1).T.astype(jnp.bfloat16)

    lax.fori_loop(q, 2 * q - 1, group, 0)

    def early_copy(k):
        return remote(
            early, early_all.at[mine], early_send.at[k], early_recv.at[mine], q + flip(mine, k, bbits)
        )

    @pl.when(is_centre)
    def _():
        own_outer, own_centre = 3 * half * q, (1 + half) * q
        far_outer, far_centre = 3 * (1 - half) * q, (2 - half) * q
        total = red[me].astype(jnp.float32)
        others = [(own_outer, j) for j in range(q)] + [(own_centre, j) for j in range(1, q)]
        others += [(far_outer, j) for j in range(q)] + [(far_centre, j) for j in range(first_late)]
        for base, j in others:
            other = base + flip(my_q, j, qbits)
            pltpu.make_async_copy(red.at[other], red.at[other], red_recv.at[other]).wait()
            total = total + red[other].astype(jnp.float32)
        early[...] = total.astype(early.dtype)
        early_all[mine] = total.astype(early.dtype)
        for k in range(blocks - 1, 0, -1):
            early_copy(k).start()

    group(2 * q - 1, 0)

    def field_copy_to(k):
        return remote(fld, fld_all.at[mine], fld_send.at[k], fld_recv.at[mine], k)

    @pl.when(is_centre)
    def _():
        for k in range(1, blocks):
            other = flip(mine, k, bbits)
            pltpu.make_async_copy(early_all.at[other], early_all.at[other], early_recv.at[other]).wait()
        dens = [early_all[block].astype(jnp.float32) for block in range(blocks)]
        for j in range(first_late, q):
            at = j - first_late
            for k in range(1, blocks):
                other = flip(mine, k, bbits)
                pltpu.make_async_copy(late.at[other, at], late.at[other, at], late_recv.at[other, at]).wait()
            for block in range(blocks):
                source = (1 - block // q) * q + flip(block % q, j, qbits)
                dens[block] = dens[block] + late[source, at].astype(jnp.float32)
        whole = jnp.concatenate(dens, axis=1).astype(jnp.bfloat16)
        got = jnp.dot(whole, scr_mixed[...], preferred_element_type=jnp.float32).astype(jnp.bfloat16)
        fld[...] = got
        fld_all[mine] = got
        for to in [*range(q), *range(3 * q, n), *range(2 * q, 3 * q), *range(q, 2 * q)]:
            @pl.when(to != me)
            def _():
                field_copy_to(to).start()

    for k in range(1, blocks):
        other = flip(mine, k, bbits)
        pltpu.make_async_copy(fld_all.at[other], fld_all.at[other], fld_recv.at[other]).wait()

    @pl.when(is_outer)
    def _():
        pltpu.make_async_copy(fld_all.at[mine], fld_all.at[mine], fld_recv.at[mine]).wait()

    for block in range(blocks):
        field_ref[:, block * 2 * rows:(block + 1) * 2 * rows] = fld_all[block].astype(jnp.float32)

    def finish(step, carry):
        hh, qq, j, direct = place(step)
        block = hh * q + qq

        @pl.when((direct == 0) & (q + block != me))
        def _():
            to_reducer(step, block).wait_send()

        @pl.when(direct == 1)
        def _():
            for k in range(1, blocks):
                to_centre(step, j, k).wait_send()

        return carry

    lax.fori_loop(0, 2 * q, finish, 0)
    for kind in KINDS:
        for j in range(1 if kind == "plane" else 0, q):
            block_to(kind, j).wait_send()
    for at, kind in enumerate(("outer", "centre", "near")):
        val_to(at, kind).wait_send()
    for k in range(1, q):
        share(k).wait_send()

    @pl.when(is_outer)
    def _():
        scr_copy.wait_send()

    @pl.when(is_centre)
    def _():
        for k in range(1, blocks):
            early_copy(k).wait_send()
        for to in range(n):
            @pl.when(to != me)
            def _():
                field_copy_to(to).wait_send()


def project_kernel(condt_ref, valt_ref, field_ref, out_hbm, held, out_sem):
    v = valt_ref.shape[0]
    batch = field_ref.shape[0]
    valt = valt_ref[...]
    copies = []
    for b in range(0, batch, 4):
        weights = jnp.concatenate(
            [valt * field_ref[b + i:b + i + 1, :].astype(jnp.bfloat16) for i in range(4)], axis=0
        )
        summed = lax.dot_general(condt_ref[...], weights, NT, preferred_element_type=jnp.float32)
        for i in range(4):
            held[b + i] = summed[:, i * v:(i + 1) * v].astype(jnp.bfloat16)
        copy = pltpu.make_async_copy(held.at[pl.ds(b, 4)], out_hbm.at[pl.ds(b, 4)], out_sem.at[b // 4])
        copy.start()
        copies.append(copy)
    for copy in copies:
        copy.wait()


def fast_body(n, excitations, valence_orb, conduction_orb, screened):
    batch, cl, v = excitations.shape
    rows, points = screened.shape
    q, first_late = n // 4, 2
    blocks, lates = 2 * q, q - first_late
    bf, f32, sent_as = jnp.bfloat16, jnp.float32, jnp.bfloat16
    hbm = pl.BlockSpec(memory_space=pltpu.HBM)
    vmem = pl.BlockSpec(memory_space=pltpu.VMEM)
    dma = pltpu.SemaphoreType.DMA
    condt, valt, field = pl.pallas_call(
        functools.partial(gather_kernel, n, first_late),
        out_shape=(
            jax.ShapeDtypeStruct((cl, points), bf),
            jax.ShapeDtypeStruct((v, points), bf),
            jax.ShapeDtypeStruct((batch, points), f32),
        ),
        in_specs=[hbm, hbm, hbm, hbm],
        out_specs=(vmem, vmem, vmem),
        scratch_shapes=[
            pltpu.VMEM((batch, cl, v), bf),
            pltpu.VMEM((batch * v, cl), bf),
            pltpu.VMEM((n, rows, cl), bf),
            pltpu.VMEM((q, 4, rows, v), bf),
            pltpu.VMEM((2, rows, points), bf),
            pltpu.VMEM((points, 2 * rows), bf),
            pltpu.VMEM((blocks, batch, 2 * rows), sent_as),
            pltpu.VMEM((n, batch, 2 * rows), sent_as),
            pltpu.VMEM((batch, 2 * rows), f32),
            pltpu.VMEM((blocks, batch, 2 * rows), f32),
            pltpu.VMEM((blocks, lates, batch, 2 * rows), sent_as),
            pltpu.VMEM((batch, 2 * rows), bf),
            pltpu.VMEM((blocks, batch, 2 * rows), bf),
            dma, dma((2,)),
            dma((n,)), dma((n,)), dma, dma, dma((3,)), dma((4,)), dma((q,)), dma((q,)),
            dma((blocks,)), dma((n,)), dma((blocks,)), dma((blocks,)),
            dma((lates, blocks)), dma((blocks, lates)), dma((n,)), dma((blocks,)),
        ],
        compiler_params=pltpu.CompilerParams(
            collective_id=0, has_side_effects=True, vmem_limit_bytes=24 * 1024 * 1024
        ),
        name="gather_field",
    )(*[pltpu.with_memory_space_constraint(x, pltpu.HBM) for x in (excitations, valence_orb, conduction_orb, screened)])
    return pl.pallas_call(
        project_kernel,
        out_shape=jax.ShapeDtypeStruct((batch, cl, v), bf),
        in_specs=[vmem, vmem, vmem],
        out_specs=hbm,
        scratch_shapes=[pltpu.VMEM((batch, cl, v), bf), dma((batch // 4,))],
        compiler_params=pltpu.CompilerParams(vmem_limit_bytes=24 * 1024 * 1024),
        name="project",
    )(condt, valt, field)


def over_blocks(total_rows, step_fn, initial):
    span_size = math.gcd(total_rows, 2048)
    block_count = total_rows // span_size
    if block_count == 1:
        return step_fn(initial, 0, span_size)
    return lax.fori_loop(
        0, block_count, lambda index, carry: step_fn(carry, index * span_size, span_size), initial
    )


def density_rows(flat_exc, batch, valence_rows, cond_rows):
    total_rows = valence_rows.shape[0]
    cond_local = cond_rows.shape[1]
    initial = jnp.zeros((batch, total_rows), jnp.float32)

    def step_fn(carry, offset, span_size):
        val_block = lax.dynamic_slice_in_dim(valence_rows, offset, span_size, 0)
        cond_block = lax.dynamic_slice_in_dim(cond_rows, offset, span_size, 0)
        mixed = lax.dot_general(
            flat_exc, val_block, (((1,), (1,)), ((), ())), preferred_element_type=jnp.float32
        )
        mixed = mixed.reshape(batch, cond_local, span_size)
        summed = jnp.sum(mixed * cond_block.T.astype(jnp.float32)[None], axis=1)
        return lax.dynamic_update_slice_in_dim(carry, summed, offset, 1)

    return over_blocks(total_rows, step_fn, initial)


def projection(carry, valence_rows, cond_rows, field_cols):
    total_rows = valence_rows.shape[0]
    batch = field_cols.shape[0]
    cond_local = cond_rows.shape[1]

    def step_fn(inner, offset, span_size):
        val_block = lax.dynamic_slice_in_dim(valence_rows, offset, span_size, 0)
        cond_block = lax.dynamic_slice_in_dim(cond_rows, offset, span_size, 0)
        field_block = lax.dynamic_slice_in_dim(field_cols, offset, span_size, 1)
        pair = (
            cond_block.T.astype(jnp.float32)[None] * field_block.astype(jnp.float32)[:, None, :]
        ).astype(jnp.bfloat16)
        pair = pair.reshape(batch * cond_local, span_size)
        return inner + jnp.dot(pair, val_block, preferred_element_type=jnp.float32)

    return over_blocks(total_rows, step_fn, carry)


def general_body(excitations, valence_orb, conduction_orb, screened):
    batch, cond_local, valence = excitations.shape
    flat_exc = excitations.reshape(batch * cond_local, valence)
    valence_whole = lax.all_gather(valence_orb, "row", axis=0, tiled=True)
    cond_rows = lax.all_to_all(conduction_orb, "row", split_axis=1, concat_axis=0, tiled=True)
    partial_density = density_rows(flat_exc, batch, valence_whole, cond_rows)
    density_whole = lax.psum(partial_density, "row").astype(jnp.bfloat16)
    field_mine = lax.dot_general(
        density_whole, screened, (((1,), (1,)), ((), ())), preferred_element_type=jnp.float32
    ).astype(jnp.bfloat16)
    initial = jnp.zeros((batch * cond_local, valence), jnp.float32)
    summed = projection(
        initial, valence_whole, cond_rows, lax.all_gather(field_mine, "row", axis=1, tiled=True)
    )
    return summed.reshape(batch, cond_local, valence).astype(jnp.bfloat16)


def body(n, excitations, valence_orb, conduction_orb, screened):
    batch, cl, v = excitations.shape
    rows = valence_orb.shape[0]
    fits = n == 16 and cl % 128 == 0 and v == 128 and rows == 64 and batch == 16
    if fits:
        return fast_body(n, excitations, valence_orb, conduction_orb, screened)
    return general_body(excitations, valence_orb, conduction_orb, screened)


def solution(mesh):
    in_specs = (
        P("grp", "row", None),
        P(("grp", "row"), None),
        P(("grp", "row"), None),
        P(("grp", "row"), None),
    )
    out_specs = P("grp", "row", None)
    return jax.shard_map(
        functools.partial(body, mesh.shape["row"]),
        mesh=mesh, in_specs=in_specs, out_specs=out_specs, check_vma=False,
    )
```
